128 devices in a mesh: layer: 16 (over y_hi, x, core), lat: 8 (over y_lo, z).
Axes of the slice: x: 4, y: 4 (y_hi: 2, y_lo: 2; y = y_hi * 2 + y_lo), z: 4, core: 2. Of those that a mesh axis runs over, the one named last changes fastest.
Arguments:
- source: float32 [16, 2, 1536, 128], P('layer', None, 'lat'), may hold values from -6 to 6
- wavenumber: float32 [16, 1536, 128], P('layer', 'lat'), may hold values from 0.1 to 1
- green_down: bfloat16 [16, 2, 1536, 3072], P('layer', None, 'lat'), may hold values from -0.109375 to 0.109375
- green_up: bfloat16 [16, 2, 1536, 3072], P('layer', None, 'lat'), may hold values from -0.109375 to 0.109375
Outputs:
- down_trace: float32 [16, 2, 1536, 128], P('layer', None, 'lat')
- up_trace: float32 [16, 2, 1536, 128], P('layer', None, 'lat')
The draws below stay inside these ranges and needn't reach their ends.
All inputs are finite; a program needn't handle non-finite values.
Results may differ from the reference program's by a relative error of at most 0.017.
Values may be sent and summed in bfloat16 or wider, within the bound.
No kernel may reach another device: no remote copies, remote signals or barrier semaphores. Data moves between devices by JAX's collectives and lax.ppermute only.
A program may use at most 64 MiB of HBM per device.

```python
import math
import jax
import jax.numpy as jnp
from jax import lax

WIDTH = 1536
ROWS = 128
RELAX = 4
LAYERS = 16


def levels(rng, dims, pieces, low, largest):
    def one(position, blocks):
        draws = jax.random.uniform(jax.random.fold_in(jax.random.fold_in(rng, 6), position), (blocks,), jnp.float32, low / len(pieces), largest / len(pieces))
        return jnp.repeat(jnp.exp(draws), dims[position] // blocks).reshape((-1,) + (1,) * (len(dims) - position - 1))

    factor_of = one(*pieces[0])
    for cut in pieces[1:]:
        factor_of = factor_of * one(*cut)
    return factor_of


def gaussian(rng, shape, width, bound, cuts=(), held_as=jnp.bfloat16):
    values = width * jax.random.normal(rng, shape, jnp.float32)
    if cuts:
        values = values * levels(rng, shape, cuts, -0.22, 0.18)
    return jnp.clip(values, -bound, bound).astype(held_as)


def setup_inputs(seed: int = 0) -> dict:
    key_list = jax.random.split(jax.random.key(seed), 5)
    source = gaussian(key_list[0], (LAYERS, 2, WIDTH, ROWS), 1.0, 6.0, ((0, 16), (2, 8)), jnp.float32)
    wavenumber = jnp.clip(jnp.exp(math.log(1.0) - 2.3025851 * jax.random.uniform(key_list[1], (LAYERS, WIDTH, ROWS), jnp.float32) ** levels(key_list[1], (LAYERS, WIDTH, ROWS), ((0, 16), (1, 8)), -0.2, 0.2)), 0.1, 1.0)
    green_down = gaussian(key_list[2], (LAYERS, 2, WIDTH, 2 * WIDTH), (2 * WIDTH) ** -0.5, 0.109375, ((0, 16), (2, 8)))
    green_up = gaussian(key_list[3], (LAYERS, 2, WIDTH, 2 * WIDTH), (2 * WIDTH) ** -0.5, 0.109375, ((0, 16), (2, 8)))
    return dict(source=source, wavenumber=wavenumber, green_down=green_down, green_up=green_up)


relax_weight = 0.8
damping = 0.5


def relax_step(field, lateral_pad, forcing, diag_real, diag_imag, inverse_real, inverse_imag):
    along = jnp.pad(field, ((0, 0), (0, 0), (1, 1)))
    beside = lateral_pad[:, 2:] + lateral_pad[:, :-2] + along[:, :, 2:] + along[:, :, :-2]
    apply_real = diag_real * field[0] - diag_imag * field[1] - beside[0]
    apply_imag = diag_real * field[1] + diag_imag * field[0] - beside[1]
    res_real = forcing[0] - apply_real
    res_imag = forcing[1] - apply_imag
    step_real = res_real * inverse_real - res_imag * inverse_imag
    step_imag = res_real * inverse_imag + res_imag * inverse_real
    return field + relax_weight * jnp.stack([step_real, step_imag], 0)


def relax(forcing, wave_sq):
    diag_real = 4.0 - wave_sq
    diag_imag = damping * wave_sq
    denom = diag_real * diag_real + diag_imag * diag_imag
    inverse_real = diag_real / denom
    inverse_imag = -diag_imag / denom
    field = jnp.zeros_like(forcing)
    for sweep in range(RELAX):
        padded = jnp.pad(field, ((0, 0), (1, 1), (0, 0)))
        field = relax_step(field, padded, forcing, diag_real, diag_imag, inverse_real, inverse_imag)
    return field


def sweep_chain(traces, green, backward):
    def turn(carry, pair):
        trace_now, block = pair
        flat = block.reshape(2 * WIDTH, 2 * WIDTH)
        incoming = carry.astype(jnp.bfloat16).reshape(2 * WIDTH, ROWS)
        product = jnp.dot(flat, incoming, preferred_element_type=jnp.float32)
        result = trace_now + product.reshape(2, WIDTH, ROWS)
        return result, result

    start = jnp.zeros((2, WIDTH, ROWS), jnp.float32)
    final, results = lax.scan(turn, start, (traces, green), reverse=backward)
    return results


def reference(source, wavenumber, green_down, green_up):
    traces = jax.vmap(relax)(source, wavenumber)
    down_trace = sweep_chain(traces, green_down, False)
    up_trace = sweep_chain(traces, green_up, True)
    return down_trace, up_trace
```

```python
import jax
import jax.numpy as jnp
import numpy as np
from jax import lax
from jax.experimental import pallas as pl
from jax.experimental.pallas import tpu as pltpu
from jax.sharding import PartitionSpec as P

RELAX = 4
LAYERS = 16
LATS = 8
HALF = LAYERS // 2
BOTH = ("layer", "lat")
SHARED = ((1, 5), (3, 7), (2, 6), (4, 12), (8,), (9, 13), (11, 15), (10, 14))
FAN = 4
CHUNKS = 4


relax_weight = 0.8
damping = 0.5


def partner_of(layer, lat):
    return lat ^ 4 if layer % 2 == 0 else lat ^ 1


def target_of(layer, lat, r):
    y, z = lat >> 2, lat & 3
    a, b = r >> 1, r & 1
    if layer % 2 == 0:
        return (((z & 1) ^ a) << 2) | (y + 2 * ((z >> 1) ^ b))
    return ((z & 1) << 2) | ((y ^ a) + 2 * ((z >> 1) ^ b))


def routes(step, r):
    steps = next(group for group in SHARED if step in group)
    edges = [e for s in steps for e in ((s - 1, s), (LAYERS - s, LAYERS - 1 - s))]
    return [
        (src * LATS + j, dst * LATS + target_of(src, j, r)) for src, dst in edges for j in range(LATS)
    ]


PAIRS = [(l * LATS + j, l * LATS + partner_of(l, j)) for l in range(LAYERS) for j in range(LATS)]


def slab_table():
    table = np.zeros((2, LATS, 2, FAN), np.int32)
    for parity in range(2):
        source = 1 - parity
        for j in range(LATS):
            for r in range(FAN):
                there = target_of(source, j, r)
                table[parity, there, 0, r] = j
                table[parity, there, 1, r] = partner_of(source, j)
    return table


def padded_2(block, axis, dim, width):
    count = lax.axis_size(axis)
    forward = [(i, i + 1) for i in range(count - 1)]
    backward = [(target, source) for source, target in forward]
    low = lax.ppermute(
        lax.slice_in_dim(block, block.shape[dim] - width, None, axis=dim), axis, forward
    )
    high = lax.ppermute(lax.slice_in_dim(block, 0, width, axis=dim), axis, backward)
    return jnp.concatenate([low, block, high], axis=dim)


def relax_step(field, lateral_pad, forcing, diag_real, diag_imag, inverse_real, inverse_imag):
    along = jnp.pad(field, ((0, 0), (0, 0), (1, 1)))
    beside = lateral_pad[:, 2:] + lateral_pad[:, :-2] + along[:, :, 2:] + along[:, :, :-2]
    apply_real = diag_real * field[0] - diag_imag * field[1] - beside[0]
    apply_imag = diag_real * field[1] + diag_imag * field[0] - beside[1]
    res_real = forcing[0] - apply_real
    res_imag = forcing[1] - apply_imag
    step_real = res_real * inverse_real - res_imag * inverse_imag
    step_imag = res_real * inverse_imag + res_imag * inverse_real
    return field + relax_weight * jnp.stack([step_real, step_imag], 0)


def coefficients(wave_sq):
    diag_real = 4.0 - wave_sq
    diag_imag = damping * wave_sq
    denom = diag_real * diag_real + diag_imag * diag_imag
    return (diag_real, diag_imag, diag_real / denom, -diag_imag / denom)


def relaxed(forcing, wave_sq):
    slab = forcing.shape[1]
    width = slab * lax.axis_size("lat")
    stacked = jnp.concatenate([forcing, wave_sq[None]], 0)
    wide = padded_2(stacked.astype(jnp.bfloat16), "lat", 1, RELAX).astype(stacked.dtype)
    wide_forcing = wide[:2]
    diag_real, diag_imag, inverse_real, inverse_imag = coefficients(wide[2])
    position = lax.axis_index("lat") * slab - RELAX + lax.iota(jnp.int32, slab + 2 * RELAX)
    inside = ((position >= 0) & (position < width)).astype(jnp.float32)[None, :, None]
    field = jnp.zeros_like(wide_forcing)
    for sweep in range(RELAX):
        padded = jnp.pad(field, ((0, 0), (1, 1), (0, 0)))
        field = (
            relax_step(
                field, padded, wide_forcing, diag_real, diag_imag, inverse_real, inverse_imag
            )
            * inside
        )
    return field[:, RELAX : RELAX + slab]


def step_kernel(info, own, other, trace, before, p0, p1, p2, p3, after, rounded, whole, total):
    slab = trace.shape[0] // 2
    half = trace.shape[1] // 2
    cells = whole.shape[0] // 2
    live = info[2 * FAN] != 0

    @pl.when(jnp.logical_not(live))
    def _():
        after[...] = before[...]
        rounded[...] = before[...].astype(jnp.bfloat16)

    @pl.when(live)
    def _():
        for r, piece in enumerate((p0, p1, p2, p3)):
            for side in range(2):
                at = pl.multiple_of(info[side * FAN + r] * slab, slab)
                block = piece[side * slab : (side + 1) * slab, :]
                whole[pl.ds(at, slab), :] = block
                turned = jnp.concatenate([block[:, half:], block[:, :half]], 1)
                whole[pl.ds(at + cells, slab), :] = turned
        total[...] = jnp.zeros_like(total)
        depth = 2 * cells // CHUNKS

        @pl.loop(0, CHUNKS)
        def _(chunk):
            at = pl.multiple_of(chunk * depth, depth)
            incoming = whole[pl.ds(at, depth), :]
            for side, green in enumerate((own, other)):
                rows = slice(2 * side * slab, 2 * (side + 1) * slab)
                flat = green[:, :, pl.ds(at, depth)].reshape(2 * slab, depth)
                total[rows, :] += jnp.dot(flat, incoming, preferred_element_type=jnp.float32)

        lane = lax.broadcasted_iota(jnp.int32, (slab, 2 * half), 1)
        for side in range(2):
            real = total[2 * side * slab : (2 * side + 1) * slab, :]
            imag = total[(2 * side + 1) * slab : (2 * side + 2) * slab, :]
            rows = slice(side * slab, (side + 1) * slab)
            value = trace[rows, :] + jnp.where(lane < half, real, pltpu.roll(imag, half, 1))
            after[rows, :] = value
            rounded[rows, :] = value.astype(jnp.bfloat16)


def one_step(info, own, other, trace, before, pieces):
    rows, lanes = trace.shape
    cells = own.shape[2] // 2
    vmem = pl.BlockSpec(memory_space=pltpu.VMEM)
    return pl.pallas_call(
        step_kernel,
        out_shape=(
            jax.ShapeDtypeStruct((rows, lanes), jnp.float32),
            jax.ShapeDtypeStruct((rows, lanes), jnp.bfloat16),
        ),
        in_specs=[pl.BlockSpec(memory_space=pltpu.SMEM)] + [vmem] * 8,
        out_specs=(vmem, vmem),
        scratch_shapes=[
            pltpu.VMEM((2 * cells, lanes), jnp.bfloat16),
            pltpu.VMEM((2 * rows, lanes), jnp.float32),
        ],
        compiler_params=pltpu.CompilerParams(vmem_limit_bytes=24 * 1024 * 1024),
        cost_estimate=pl.CostEstimate(
            flops=4 * rows * 2 * cells * lanes, bytes_accessed=2 * own.size * 2, transcendentals=0
        ),
    )(info, own, other, trace, before, *pieces)


def local(source, wavenumber, green_down, green_up):
    layer = lax.axis_index("layer")
    lat = lax.axis_index("lat")
    low = layer < HALF
    parity = layer % 2
    upper = jnp.where(parity == 0, lat // 4, lat % 2) == 1
    depth = jnp.minimum(layer, LAYERS - 1 - layer)
    slabs = jnp.asarray(slab_table().reshape(2 * LATS, 2 * FAN))
    mine = lax.dynamic_index_in_dim(slabs, parity * LATS + lat, 0, keepdims=False)

    own_first = jnp.where(low, green_down[0], green_up[0])
    other_first = lax.ppermute(own_first, BOTH, PAIRS)
    own_second = jnp.where(low, green_up[0], green_down[0])
    ready, other_first = lax.optimization_barrier((own_second, other_first))
    other_second = lax.ppermute(ready, BOTH, PAIRS)

    traces = relaxed(source[0], wavenumber[0])
    half = traces.shape[2] // 2

    def packed(part):
        columns = slice(part * half, (part + 1) * half)
        return jnp.concatenate([traces[0, :, columns], traces[1, :, columns]], 1)

    keep = jnp.where(upper, packed(1), packed(0))
    give = jnp.where(upper, packed(0), packed(1))
    trace = jnp.concatenate([keep, lax.ppermute(give, BOTH, PAIRS)], 0)

    def advance(step, when, own, other, before, sent):
        pieces = [lax.ppermute(sent, BOTH, routes(step, r)) for r in range(FAN)]
        live = (when == step).astype(jnp.int32)
        info = jnp.concatenate([mine, live[None]])
        return one_step(info, own, other, trace, before, pieces)

    first, sent = trace, trace.astype(jnp.bfloat16)
    for step in range(1, HALF):
        first, sent = advance(step, depth, own_first, other_first, first, sent)
    second = trace
    for step in range(HALF, LAYERS):
        second, sent = advance(step, LAYERS - 1 - depth, own_second, other_second, second, sent)

    slab = traces.shape[1]
    done = jnp.stack([first, second], 0)
    held = done[:, :slab]
    got = lax.ppermute(done[:, slab:], BOTH, PAIRS)
    left = jnp.where(upper, got, held)
    right = jnp.where(upper, held, got)
    real = jnp.concatenate([left[:, :, :half], right[:, :, :half]], 2)
    imag = jnp.concatenate([left[:, :, half:], right[:, :, half:]], 2)
    both = jnp.stack([real, imag], 1)
    down = jnp.where(low, both[0], both[1])
    up = jnp.where(low, both[1], both[0])
    return (down[None], up[None])


def solution(mesh):
    return jax.shard_map(
        local,
        mesh=mesh,
        in_specs=(
            P("layer", None, "lat", None),
            P("layer", "lat", None),
            P("layer", None, "lat", None),
            P("layer", None, "lat", None),
        ),
        out_specs=(P("layer", None, "lat", None), P("layer", None, "lat", None)),
        check_vma=False,
    )
```

```python
import functools

import jax
import jax.numpy as jnp
import numpy as np
from jax import lax
from jax.experimental import pallas as pl
from jax.experimental.pallas import tpu as pltpu
from jax.sharding import PartitionSpec as P

RELAX = 4
LAYERS = 16
LATS = 8
HALF = LAYERS // 2
BOTH = ("layer", "lat")
SHARED = ((1, 5), (2, 6), (3, 7), (4, 9), (10, 13), (11, 14), (12, 15))
FAN = 4
BATCHES = ((3, 2, 1), (0,))


relax_weight = 0.8
damping = 0.5


def partner_of(layer, lat):
    return lat ^ 4 if layer % 2 == 0 else lat ^ 1


def target_of(layer, lat, r):
    y, z = lat >> 2, lat & 3
    a, b = r >> 1, r & 1
    if layer % 2 == 0:
        return (((z & 1) ^ a) << 2) | (y + 2 * ((z >> 1) ^ b))
    return ((z & 1) << 2) | ((y ^ a) + 2 * ((z >> 1) ^ b))


def edges_of(step):
    return [(step - 1, step), (LAYERS - step, LAYERS - 1 - step)]


def routes(step, r):
    steps = next(group for group in SHARED if step in group)
    edges = [edge for s in steps for edge in edges_of(s)]
    return [
        (src * LATS + j, dst * LATS + target_of(src, j, r)) for src, dst in edges for j in range(LATS)
    ]


def spread(step, r):
    return [
        (dst * LATS + j, dst * LATS + target_of(src, j, r))
        for src, dst in edges_of(step)
        for j in range(LATS)
    ]


def straight(step):
    return [(src * LATS + j, dst * LATS + j) for src, dst in edges_of(step) for j in range(LATS)]


PAIRS = [(l * LATS + j, l * LATS + partner_of(l, j)) for l in range(LAYERS) for j in range(LATS)]


def rank_table():
    table = np.zeros((2, LATS, FAN), np.int32)
    for parity in range(2):
        source = 1 - parity
        for j in range(LATS):
            pair = j % 4 if source % 2 == 0 else j // 2
            for r in range(FAN):
                table[parity, target_of(source, j, r), pair] = r
    return table


def padded_2(block, axis, dim, width):
    count = lax.axis_size(axis)
    forward = [(i, i + 1) for i in range(count - 1)]
    backward = [(target, source) for source, target in forward]
    low = lax.ppermute(
        lax.slice_in_dim(block, block.shape[dim] - width, None, axis=dim), axis, forward
    )
    high = lax.ppermute(lax.slice_in_dim(block, 0, width, axis=dim), axis, backward)
    return jnp.concatenate([low, block, high], axis=dim)


def relax_step(field, lateral_pad, forcing, diag_real, diag_imag, inverse_real, inverse_imag):
    along = jnp.pad(field, ((0, 0), (0, 0), (1, 1)))
    beside = lateral_pad[:, 2:] + lateral_pad[:, :-2] + along[:, :, 2:] + along[:, :, :-2]
    apply_real = diag_real * field[0] - diag_imag * field[1] - beside[0]
    apply_imag = diag_real * field[1] + diag_imag * field[0] - beside[1]
    res_real = forcing[0] - apply_real
    res_imag = forcing[1] - apply_imag
    step_real = res_real * inverse_real - res_imag * inverse_imag
    step_imag = res_real * inverse_imag + res_imag * inverse_real
    return field + relax_weight * jnp.stack([step_real, step_imag], 0)


def coefficients(wave_sq):
    diag_real = 4.0 - wave_sq
    diag_imag = damping * wave_sq
    denom = diag_real * diag_real + diag_imag * diag_imag
    return (diag_real, diag_imag, diag_real / denom, -diag_imag / denom)


def relaxed(forcing, wave_sq):
    slab = forcing.shape[1]
    width = slab * lax.axis_size("lat")
    stacked = jnp.concatenate([forcing, wave_sq[None]], 0)
    wide = padded_2(stacked.astype(jnp.bfloat16), "lat", 1, RELAX).astype(stacked.dtype)
    wide_forcing = wide[:2]
    diag_real, diag_imag, inverse_real, inverse_imag = coefficients(wide[2])
    position = lax.axis_index("lat") * slab - RELAX + lax.iota(jnp.int32, slab + 2 * RELAX)
    inside = ((position >= 0) & (position < width)).astype(jnp.float32)[None, :, None]
    field = jnp.zeros_like(wide_forcing)
    for sweep in range(RELAX):
        padded = jnp.pad(field, ((0, 0), (1, 1), (0, 0)))
        field = (
            relax_step(
                field, padded, wide_forcing, diag_real, diag_imag, inverse_real, inverse_imag
            )
            * inside
        )
    return field[:, RELAX : RELAX + slab]


def load_kernel(info, own, other, out, first, second, sems):
    slab = first.shape[1]
    cells = first.shape[2] // 2
    copies = [
        pltpu.make_async_copy(own, first, sems.at[0]),
        pltpu.make_async_copy(other, second, sems.at[1]),
    ]
    for copy in copies:
        copy.start()
    for copy in copies:
        copy.wait()
    even = info[FAN] == 0
    band = slab // 3

    @pl.loop(0, 6)
    def _(step):
        part = lax.div(step, 3)
        start = lax.rem(step, 3) * band
        near = pl.ds(pl.multiple_of(start, band), band)
        for held, green in ((info[FAN + 1], first), (1 - info[FAN + 1], second)):
            base = held * 2 * slab + part * slab + start
            rows = pl.ds(pl.multiple_of(base, band), band)

            @pl.when(even)
            def _():
                for pair in range(FAN):
                    for column in range(2):
                        at = column * cells + pair * 2 * slab
                        out[info[pair], rows, column * 2 * slab : (column + 1) * 2 * slab] = green[
                            part, near, at : at + 2 * slab
                        ]

            @pl.when(jnp.logical_not(even))
            def _():
                for pair in range(FAN):
                    for column in range(2):
                        low = column * cells + pair * slab
                        high = low + cells // 2
                        left = green[part, near, low : low + slab]
                        right = green[part, near, high : high + slab]
                        out[info[pair], rows, column * 2 * slab : (column + 1) * 2 * slab] = (
                            jnp.concatenate([left, right], 1)
                        )


def loaded(info, own, other):
    slab, cells = own.shape[1], own.shape[2] // 2
    anywhere = pl.BlockSpec(memory_space=pl.ANY)
    return pl.pallas_call(
        load_kernel,
        out_shape=jax.ShapeDtypeStruct((FAN, 4 * slab, 2 * cells // FAN), own.dtype),
        in_specs=[pl.BlockSpec(memory_space=pltpu.SMEM), anywhere, anywhere],
        out_specs=pl.BlockSpec(memory_space=pltpu.VMEM),
        scratch_shapes=[
            pltpu.VMEM(own.shape, own.dtype),
            pltpu.VMEM(own.shape, own.dtype),
            pltpu.SemaphoreType.DMA((2,)),
        ],
        compiler_params=pltpu.CompilerParams(vmem_limit_bytes=16 * 1024 * 1024),
        cost_estimate=pl.CostEstimate(
            flops=0, bytes_accessed=8 * own.size, transcendentals=0
        ),
    )(info, own, other)


def product(batch, green, pieces, whole, total):
    cells, lanes = pieces[0].shape
    half = lanes // 2
    for k, piece in enumerate(pieces):
        block = piece[...]
        whole[2 * k] = block
        whole[2 * k + 1] = jnp.concatenate([block[:, half:], block[:, :half]], 1)
    total[...] = jnp.zeros_like(total)

    @pl.loop(0, 2 * len(batch))
    def _(k):
        r = batch[0] - lax.div(k, 2)
        at = pl.multiple_of(lax.rem(k, 2) * cells, cells)
        flat = green[r, :, pl.ds(at, cells)]
        total[...] += jnp.dot(flat, whole[k], preferred_element_type=jnp.float32)


def early_kernel(batch, flag, info, green, *refs):
    pieces, (total, whole) = refs[:-2], refs[-2:]

    @pl.when(info[flag] != 0)
    def _():
        product(batch, green, pieces, whole, total)


def late_kernel(batch, flag, info, green, trace, before, sent, total, *refs):
    pieces, (after, rounded, whole, rest) = refs[: len(batch)], refs[len(batch) :]
    slab = trace.shape[0] // 2
    half = trace.shape[1] // 2

    @pl.when(info[flag] != 0)
    def _():
        product(batch, green, pieces, whole, rest)
        lane = lax.broadcasted_iota(jnp.int32, (slab, 2 * half), 1)
        for side in range(2):
            upper = slice(2 * side * slab, (2 * side + 1) * slab)
            lower = slice((2 * side + 1) * slab, (2 * side + 2) * slab)
            real = total[upper, :] + rest[upper, :]
            imag = total[lower, :] + rest[lower, :]
            rows = slice(side * slab, (side + 1) * slab)
            value = trace[rows, :] + jnp.where(lane < half, real, pltpu.roll(imag, half, 1))
            after[rows, :] = value
            rounded[rows, :] = value.astype(jnp.bfloat16)

    @pl.when(info[flag] == 0)
    def _():
        after[...] = before[...]
        rounded[...] = sent[...]


def one_step(step, info, green, trace, before, sent, pieces):
    flag = FAN + 1 + step
    rows, lanes = trace.shape
    vmem = pl.BlockSpec(memory_space=pltpu.VMEM)
    smem = pl.BlockSpec(memory_space=pltpu.SMEM)
    early, late = BATCHES
    params = pltpu.CompilerParams(vmem_limit_bytes=8 * 1024 * 1024)

    def cost(batch):
        work = 2 * green.shape[1] * green.shape[2] * lanes * len(batch)
        return pl.CostEstimate(flops=work, bytes_accessed=work // 128, transcendentals=0)

    total = pl.pallas_call(
        functools.partial(early_kernel, early, flag),
        out_shape=jax.ShapeDtypeStruct((2 * rows, lanes), jnp.float32),
        in_specs=[smem] + [vmem] * (1 + len(early)),
        out_specs=vmem,
        scratch_shapes=[pltpu.VMEM((2 * len(early), rows, lanes), jnp.bfloat16)],
        compiler_params=params,
        cost_estimate=cost(early),
    )(info, green, *[pieces[r] for r in early])
    return pl.pallas_call(
        functools.partial(late_kernel, late, flag),
        out_shape=(
            jax.ShapeDtypeStruct((rows, lanes), jnp.float32),
            jax.ShapeDtypeStruct((rows, lanes), jnp.bfloat16),
        ),
        in_specs=[smem] + [vmem] * (5 + len(late)),
        out_specs=(vmem, vmem),
        scratch_shapes=[
            pltpu.VMEM((2 * len(late), rows, lanes), jnp.bfloat16),
            pltpu.VMEM((2 * rows, lanes), jnp.float32),
        ],
        compiler_params=params,
        cost_estimate=cost(late),
    )(info, green, trace, before, sent, total, *[pieces[r] for r in late])


def local(source, wavenumber, green_down, green_up):
    layer = lax.axis_index("layer")
    lat = lax.axis_index("lat")
    low = layer < HALF
    parity = layer & 1
    place = jnp.where(parity == 0, lat >> 2, lat & 1)
    upper = place == 1
    depth = jnp.minimum(layer, LAYERS - 1 - layer)
    ranks = jnp.asarray(rank_table().reshape(2 * LATS, FAN))
    mine = lax.dynamic_index_in_dim(ranks, parity * LATS + lat, 0, keepdims=False)
    steps = jnp.arange(1, LAYERS)
    live = ((steps == depth) | (steps == LAYERS - 1 - depth)).astype(jnp.int32)
    info = jnp.concatenate([mine, jnp.stack([parity, place]), live])

    own_first = jnp.where(low, green_down[0], green_up[0])
    other_first = lax.ppermute(own_first, BOTH, PAIRS)

    traces = relaxed(source[0], wavenumber[0])
    half = traces.shape[2] // 2

    def packed(part):
        columns = slice(part * half, (part + 1) * half)
        return jnp.concatenate([traces[0, :, columns], traces[1, :, columns]], 1)

    keep = jnp.where(upper, packed(1), packed(0))
    give = jnp.where(upper, packed(0), packed(1))
    swapped = lax.ppermute(give, BOTH, PAIRS)
    trace = jnp.where(
        upper, jnp.concatenate([swapped, keep], 0), jnp.concatenate([keep, swapped], 0)
    )
    green_first = loaded(info, own_first, other_first)

    own_second = jnp.where(low, green_up[0], green_down[0])
    own_second, other_first, trace = lax.optimization_barrier((own_second, other_first, trace))
    other_second = lax.ppermute(own_second, BOTH, PAIRS)
    green_second = loaded(info, own_second, other_second)

    def advance(step, green, before, sent):
        if step == HALF:
            shifted = lax.ppermute(sent, BOTH, straight(step))
            pieces = [lax.ppermute(shifted, BOTH, spread(step, r)) for r in range(FAN)]
        else:
            pieces = [lax.ppermute(sent, BOTH, routes(step, r)) for r in range(FAN)]
        return one_step(step, info, green, trace, before, sent, pieces)

    slab = traces.shape[1]

    def joined(done):
        held = jnp.where(upper, done[slab:], done[:slab])
        got = lax.ppermute(jnp.where(upper, done[:slab], done[slab:]), BOTH, PAIRS)
        left = jnp.where(upper, got, held)
        right = jnp.where(upper, held, got)
        real = jnp.concatenate([left[:, :half], right[:, :half]], 1)
        imag = jnp.concatenate([left[:, half:], right[:, half:]], 1)
        return jnp.stack([real, imag], 0)

    first, sent = trace, trace.astype(jnp.bfloat16)
    for step in range(1, HALF):
        first, sent = advance(step, green_first, first, sent)
    near = joined(first)
    second = trace
    for step in range(HALF, LAYERS):
        second, sent = advance(step, green_second, second, sent)
    far = joined(second)
    down = jnp.where(low, near, far)
    up = jnp.where(low, far, near)
    return (down[None], up[None])


def solution(mesh):
    return jax.shard_map(
        local,
        mesh=mesh,
        in_specs=(
            P("layer", None, "lat", None),
            P("layer", "lat", None),
            P("layer", None, "lat", None),
            P("layer", None, "lat", None),
        ),
        out_specs=(P("layer", None, "lat", None), P("layer", None, "lat", None)),
        check_vma=False,
    )
```

```python
import functools

import jax
import jax.numpy as jnp
import numpy as np
from jax import lax
from jax.experimental import pallas as pl
from jax.experimental.pallas import tpu as pltpu
from jax.sharding import PartitionSpec as P


RELAX = 4
LAYERS = 16
LATS = 8
HALF = LAYERS // 2
BOTH = ("layer", "lat")
SHARED = ((1, 5), (2, 6), (3, 7), (4, 9), (10, 13), (11, 14), (12, 15))
FAN = 4
SWAP = 6
BATCHES = ((3, 1), (0,), (2,))


relax_weight = 0.8
damping = 0.5


def partner_of(layer, lat):
    return lat ^ 4 if layer % 2 == 0 else lat ^ 1


def target_of(layer, lat, r):
    y, z = lat >> 2, lat & 3
    a, b = r >> 1, r & 1
    if layer % 2 == 0:
        return (((z & 1) ^ a) << 2) | (y + 2 * ((z >> 1) ^ b))
    return ((z & 1) << 2) | ((y ^ a) + 2 * ((z >> 1) ^ b))


def edges_of(step):
    return [(step - 1, step), (LAYERS - step, LAYERS - 1 - step)]


def routes(step, r):
    steps = next(group for group in SHARED if step in group)
    edges = [edge for s in steps for edge in edges_of(s)]
    return [
        (src * LATS + j, dst * LATS + target_of(src, j, r)) for src, dst in edges for j in range(LATS)
    ]


def spread(step, r):
    return [
        (dst * LATS + j, dst * LATS + target_of(src, j, r))
        for src, dst in edges_of(step)
        for j in range(LATS)
    ]


def straight(step):
    return [(src * LATS + j, dst * LATS + j) for src, dst in edges_of(step) for j in range(LATS)]


PAIRS = [(l * LATS + j, l * LATS + partner_of(l, j)) for l in range(LAYERS) for j in range(LATS)]


def rank_table():
    table = np.zeros((2, LATS, FAN), np.int32)
    for parity in range(2):
        source = 1 - parity
        for j in range(LATS):
            pair = j % 4 if source % 2 == 0 else j // 2
            for r in range(FAN):
                table[parity, target_of(source, j, r), pair] = r
    return table


def padded_2(block, axis, dim, width):
    count = lax.axis_size(axis)
    forward = [(i, i + 1) for i in range(count - 1)]
    backward = [(target, source) for source, target in forward]
    last = lax.slice_in_dim(block, block.shape[dim] - width, None, axis=dim)
    low = lax.ppermute(last, axis, forward)
    high = lax.ppermute(lax.slice_in_dim(block, 0, width, axis=dim), axis, backward)
    return jnp.concatenate([low, block, high], axis=dim)


def relax_step(field, lateral_pad, forcing, diag_real, diag_imag, inverse_real, inverse_imag):
    along = jnp.pad(field, ((0, 0), (0, 0), (1, 1)))
    beside = lateral_pad[:, 2:] + lateral_pad[:, :-2] + along[:, :, 2:] + along[:, :, :-2]
    apply_real = diag_real * field[0] - diag_imag * field[1] - beside[0]
    apply_imag = diag_real * field[1] + diag_imag * field[0] - beside[1]
    res_real = forcing[0] - apply_real
    res_imag = forcing[1] - apply_imag
    step_real = res_real * inverse_real - res_imag * inverse_imag
    step_imag = res_real * inverse_imag + res_imag * inverse_real
    return field + relax_weight * jnp.stack([step_real, step_imag], 0)


def coefficients(wave_sq):
    diag_real = 4.0 - wave_sq
    diag_imag = damping * wave_sq
    denom = diag_real * diag_real + diag_imag * diag_imag
    return (diag_real, diag_imag, diag_real / denom, -diag_imag / denom)


def relaxed(forcing, wave_sq):
    slab = forcing.shape[1]
    width = slab * lax.axis_size("lat")
    stacked = jnp.concatenate([forcing, wave_sq[None]], 0)
    wide = padded_2(stacked.astype(jnp.bfloat16), "lat", 1, RELAX).astype(stacked.dtype)
    wide_forcing = wide[:2]
    diag_real, diag_imag, inverse_real, inverse_imag = coefficients(wide[2])
    position = lax.axis_index("lat") * slab - RELAX + lax.iota(jnp.int32, slab + 2 * RELAX)
    inside = ((position >= 0) & (position < width)).astype(jnp.float32)[None, :, None]
    field = jnp.zeros_like(wide_forcing)
    for _ in range(RELAX):
        padded = jnp.pad(field, ((0, 0), (1, 1), (0, 0)))
        field = (
            relax_step(
                field, padded, wide_forcing, diag_real, diag_imag, inverse_real, inverse_imag
            )
            * inside
        )
    return field[:, RELAX : RELAX + slab]


def load_kernel(info, own, other, out, first, second, sems):
    slab = first.shape[1]
    cells = first.shape[2] // 2
    copies = [
        pltpu.make_async_copy(own, first, sems.at[0]),
        pltpu.make_async_copy(other, second, sems.at[1]),
    ]
    for copy in copies:
        copy.start()
    for copy in copies:
        copy.wait()
    even = info[FAN] == 0
    band = slab // 3

    @pl.loop(0, 6)
    def _(step):
        part = lax.div(step, 3)
        start = lax.rem(step, 3) * band
        near = pl.ds(pl.multiple_of(start, band), band)
        for held, green in ((info[FAN + 1], first), (1 - info[FAN + 1], second)):
            base = held * 2 * slab + part * slab + start
            rows = pl.ds(pl.multiple_of(base, band), band)

            @pl.when(even)
            def _():
                for pair in range(FAN):
                    for column in range(2):
                        at = column * cells + pair * 2 * slab
                        out[info[pair], rows, column * 2 * slab : (column + 1) * 2 * slab] = green[
                            part, near, at : at + 2 * slab
                        ]

            @pl.when(jnp.logical_not(even))
            def _():
                for pair in range(FAN):
                    for column in range(2):
                        low = column * cells + pair * slab
                        high = low + cells // 2
                        left = green[part, near, low : low + slab]
                        right = green[part, near, high : high + slab]
                        out[info[pair], rows, column * 2 * slab : (column + 1) * 2 * slab] = (
                            jnp.concatenate([left, right], 1)
                        )


def loaded(info, own, other):
    slab, cells = own.shape[1], own.shape[2] // 2
    anywhere = pl.BlockSpec(memory_space=pl.ANY)
    return pl.pallas_call(
        load_kernel,
        out_shape=jax.ShapeDtypeStruct((FAN, 4 * slab, 2 * cells // FAN), own.dtype),
        in_specs=[pl.BlockSpec(memory_space=pltpu.SMEM), anywhere, anywhere],
        out_specs=pl.BlockSpec(memory_space=pltpu.VMEM),
        scratch_shapes=[
            pltpu.VMEM(own.shape, own.dtype),
            pltpu.VMEM(own.shape, own.dtype),
            pltpu.SemaphoreType.DMA((2,)),
        ],
        compiler_params=pltpu.CompilerParams(vmem_limit_bytes=16 * 1024 * 1024),
        cost_estimate=pl.CostEstimate(
            flops=0, bytes_accessed=8 * own.size, transcendentals=0
        ),
    )(info, own, other)


def is_live(step):
    layer = lax.axis_index("layer")
    return jnp.logical_or(layer == step, layer == LAYERS - 1 - step)


def product(batch, green, pieces, whole, total, sums):
    cells, lanes = pieces[0].shape
    half = lanes // 2
    for k, piece in enumerate(pieces):
        block = piece[...]
        whole[k, :cells] = block
        whole[k, cells:] = jnp.concatenate([block[:, half:], block[:, :half]], 1)
    rows = total.shape[0] // 2

    @pl.loop(0, 2)
    def _(part):
        at = pl.ds(pl.multiple_of(part * rows, rows), rows)
        terms = [part[at, :] for part in sums]
        for k, r in enumerate(batch):
            terms.append(jnp.dot(green[r, at, :], whole[k], preferred_element_type=jnp.float32))
        total[at, :] = functools.reduce(jnp.add, terms)


def early_kernel(batch, step, green, *refs):
    pieces, sums, (total, whole) = refs[: len(batch)], refs[len(batch) : -2], refs[-2:]

    @pl.when(is_live(step))
    def _():
        product(batch, green, pieces, whole, total, sums)


def late_kernel(batch, step, green, trace, before, sent, earlier, *refs):
    pieces, (after, rounded, whole, rest) = refs[: len(batch)], refs[len(batch) :]
    slab = trace.shape[0] // 2
    half = trace.shape[1] // 2

    @pl.when(is_live(step))
    def _():
        product(batch, green, pieces, whole, rest, (earlier,))
        lane = lax.broadcasted_iota(jnp.int32, (slab, 2 * half), 1)
        for side in range(2):
            rows = slice(side * slab, (side + 1) * slab)
            real = rest[2 * side * slab : (2 * side + 1) * slab, :]
            imag = rest[(2 * side + 1) * slab : (2 * side + 2) * slab, :]
            value = trace[rows, :] + jnp.where(lane < half, real, pltpu.roll(imag, half, 1))
            after[rows, :] = value
            rounded[rows, :] = value.astype(jnp.bfloat16)

    @pl.when(jnp.logical_not(is_live(step)))
    def _():
        after[...] = before[...]
        rounded[...] = sent[...]


def one_step(step, green, trace, before, sent, pieces):
    rows, lanes = trace.shape
    vmem = pl.BlockSpec(memory_space=pltpu.VMEM)
    *early, late = BATCHES
    params = pltpu.CompilerParams(vmem_limit_bytes=8 * 1024 * 1024)

    def cost(batch):
        work = 2 * green.shape[1] * green.shape[2] * lanes * len(batch)
        return pl.CostEstimate(flops=work, bytes_accessed=work // 128, transcendentals=0)

    def held(batch):
        return pltpu.VMEM((len(batch), 2 * rows, lanes), jnp.bfloat16)

    sums = []
    for batch in early:
        total = pl.pallas_call(
            functools.partial(early_kernel, batch, step),
            out_shape=jax.ShapeDtypeStruct((2 * rows, lanes), jnp.float32),
            in_specs=[vmem] * (1 + len(batch) + len(sums)),
            out_specs=vmem,
            scratch_shapes=[held(batch)],
            compiler_params=params,
            cost_estimate=cost(batch),
        )(green, *[pieces[r] for r in batch], *sums)
        sums = [total]
    return pl.pallas_call(
        functools.partial(late_kernel, late, step),
        out_shape=(
            jax.ShapeDtypeStruct((rows, lanes), jnp.float32),
            jax.ShapeDtypeStruct((rows, lanes), jnp.bfloat16),
        ),
        in_specs=[vmem] * (5 + len(late)),
        out_specs=(vmem, vmem),
        scratch_shapes=[held(late), pltpu.VMEM((2 * rows, lanes), jnp.float32)],
        compiler_params=params,
        cost_estimate=cost(late),
    )(green, trace, before, sent, *sums, *[pieces[r] for r in late])


def local(source, wavenumber, green_down, green_up):
    layer = lax.axis_index("layer")
    lat = lax.axis_index("lat")
    low = layer < HALF
    parity = layer & 1
    place = jnp.where(parity == 0, lat >> 2, lat & 1)
    upper = place == 1
    ranks = jnp.asarray(rank_table().reshape(2 * LATS, FAN))
    mine = lax.dynamic_index_in_dim(ranks, parity * LATS + lat, 0, keepdims=False)
    info = jnp.concatenate([mine, jnp.stack([parity, place])])

    own_first = jnp.where(low, green_down[0], green_up[0])
    own_first, source, wavenumber = lax.optimization_barrier((own_first, source, wavenumber))
    other_first = lax.ppermute(own_first, BOTH, PAIRS)

    traces = relaxed(source[0], wavenumber[0])
    half = traces.shape[2] // 2

    def packed(part):
        columns = slice(part * half, (part + 1) * half)
        return jnp.concatenate([traces[0, :, columns], traces[1, :, columns]], 1)

    keep = jnp.where(upper, packed(1), packed(0))
    give = jnp.where(upper, packed(0), packed(1))
    swapped = lax.ppermute(give, BOTH, PAIRS)
    trace = jnp.where(
        upper, jnp.concatenate([swapped, keep], 0), jnp.concatenate([keep, swapped], 0)
    )
    green_first = loaded(info, own_first, other_first)

    def advance(step, green, before, sent):
        if step == HALF:
            shifted = lax.ppermute(sent, BOTH, straight(step))
            pieces = [lax.ppermute(shifted, BOTH, spread(step, r)) for r in range(FAN)]
        else:
            pieces = [lax.ppermute(sent, BOTH, routes(step, r)) for r in range(FAN)]
        return one_step(step, green, trace, before, sent, pieces)

    slab = traces.shape[1]

    def joined(done):
        held = jnp.where(upper, done[slab:], done[:slab])
        got = lax.ppermute(jnp.where(upper, done[:slab], done[slab:]), BOTH, PAIRS)
        left = jnp.where(upper, got, held)
        right = jnp.where(upper, held, got)
        real = jnp.concatenate([left[:, :half], right[:, :half]], 1)
        imag = jnp.concatenate([left[:, half:], right[:, half:]], 1)
        return jnp.stack([real, imag], 0)

    first, sent = trace, trace.astype(jnp.bfloat16)
    for step in range(1, HALF):
        if step == SWAP:
            down_later, up_later, sent = lax.optimization_barrier((green_down, green_up, sent))
            own_second = jnp.where(low, up_later[0], down_later[0])
            other_second = lax.ppermute(own_second, BOTH, PAIRS)
        first, sent = advance(step, green_first, first, sent)
    green_second = loaded(info, own_second, other_second)
    near = joined(first)
    second = trace
    for step in range(HALF, LAYERS):
        second, sent = advance(step, green_second, second, sent)
    far = joined(second)
    down = jnp.where(low, near, far)
    up = jnp.where(low, far, near)
    return (down[None], up[None])


def solution(mesh):
    return jax.shard_map(
        local,
        mesh=mesh,
        in_specs=(
            P("layer", None, "lat", None),
            P("layer", "lat", None),
            P("layer", None, "lat", None),
            P("layer", None, "lat", None),
        ),
        out_specs=(P("layer", None, "lat", None), P("layer", None, "lat", None)),
        check_vma=False,
    )
```

```python
import functools

import jax
import jax.numpy as jnp
import numpy as np
from jax import lax
from jax.experimental import pallas as pl
from jax.experimental.pallas import tpu as pltpu
from jax.sharding import PartitionSpec as P


RELAX = 4
LAYERS = 16
LATS = 8
HALF = LAYERS // 2
BOTH = ("layer", "lat")
SHARED = ((1, 5), (2, 6), (3, 7, 11), (4, 9, 14), (10, 13), (12, 15))
FAN = 4
SWAP = 6
BATCHES = ((3, 1), (0,), (2,))


relax_weight = 0.8
damping = 0.5


def partner_of(layer, lat):
    return lat ^ 4 if layer % 2 == 0 else lat ^ 1


def target_of(layer, lat, r):
    y, z = lat >> 2, lat & 3
    a, b = r >> 1, r & 1
    if layer % 2 == 0:
        return (((z & 1) ^ a) << 2) | (y + 2 * ((z >> 1) ^ b))
    return ((z & 1) << 2) | ((y ^ a) + 2 * ((z >> 1) ^ b))


def edges_of(step):
    return [(step - 1, step), (LAYERS - step, LAYERS - 1 - step)]


def routes(step, r):
    steps = next(group for group in SHARED if step in group)
    edges = [edge for s in steps for edge in edges_of(s)]
    return [
        (src * LATS + j, dst * LATS + target_of(src, j, r)) for src, dst in edges for j in range(LATS)
    ]


def spread(step, r):
    return [
        (dst * LATS + j, dst * LATS + target_of(src, j, r))
        for src, dst in edges_of(step)
        for j in range(LATS)
    ]


def straight(step):
    return [(src * LATS + j, dst * LATS + j) for src, dst in edges_of(step) for j in range(LATS)]


PAIRS = [(l * LATS + j, l * LATS + partner_of(l, j)) for l in range(LAYERS) for j in range(LATS)]


INNER_PAIRS = [pair for pair in PAIRS if 0 < pair[0] // LATS < LAYERS - 1]


def rank_table():
    table = np.zeros((2, LATS, FAN), np.int32)
    for parity in range(2):
        source = 1 - parity
        for j in range(LATS):
            pair = j % 4 if source % 2 == 0 else j // 2
            for r in range(FAN):
                table[parity, target_of(source, j, r), pair] = r
    return table


def padded_2(block, axis, dim, width):
    count = lax.axis_size(axis)
    forward = [(i, i + 1) for i in range(count - 1)]
    backward = [(target, source) for source, target in forward]
    last = lax.slice_in_dim(block, block.shape[dim] - width, None, axis=dim)
    low = lax.ppermute(last, axis, forward)
    high = lax.ppermute(lax.slice_in_dim(block, 0, width, axis=dim), axis, backward)
    return jnp.concatenate([low, block, high], axis=dim)


def relax_step(field, lateral_pad, forcing, diag_real, diag_imag, inverse_real, inverse_imag):
    along = jnp.pad(field, ((0, 0), (0, 0), (1, 1)))
    beside = lateral_pad[:, 2:] + lateral_pad[:, :-2] + along[:, :, 2:] + along[:, :, :-2]
    apply_real = diag_real * field[0] - diag_imag * field[1] - beside[0]
    apply_imag = diag_real * field[1] + diag_imag * field[0] - beside[1]
    res_real = forcing[0] - apply_real
    res_imag = forcing[1] - apply_imag
    step_real = res_real * inverse_real - res_imag * inverse_imag
    step_imag = res_real * inverse_imag + res_imag * inverse_real
    return field + relax_weight * jnp.stack([step_real, step_imag], 0)


def coefficients(wave_sq):
    diag_real = 4.0 - wave_sq
    diag_imag = damping * wave_sq
    denom = diag_real * diag_real + diag_imag * diag_imag
    return (diag_real, diag_imag, diag_real / denom, -diag_imag / denom)


def relaxed(forcing, wave_sq):
    slab = forcing.shape[1]
    width = slab * lax.axis_size("lat")
    stacked = jnp.concatenate([forcing, wave_sq[None]], 0)
    wide = padded_2(stacked.astype(jnp.bfloat16), "lat", 1, RELAX).astype(stacked.dtype)
    wide_forcing = wide[:2]
    diag_real, diag_imag, inverse_real, inverse_imag = coefficients(wide[2])
    position = lax.axis_index("lat") * slab - RELAX + lax.iota(jnp.int32, slab + 2 * RELAX)
    inside = ((position >= 0) & (position < width)).astype(jnp.float32)[None, :, None]
    field = jnp.zeros_like(wide_forcing)
    for _ in range(RELAX):
        padded = jnp.pad(field, ((0, 0), (1, 1), (0, 0)))
        field = (
            relax_step(
                field, padded, wide_forcing, diag_real, diag_imag, inverse_real, inverse_imag
            )
            * inside
        )
    return field[:, RELAX : RELAX + slab]


def load_kernel(info, own, other, out, first, second, sems):
    slab = first.shape[1]
    cells = first.shape[2] // 2
    copies = [
        pltpu.make_async_copy(own, first, sems.at[0]),
        pltpu.make_async_copy(other, second, sems.at[1]),
    ]
    for copy in copies:
        copy.start()
    for copy in copies:
        copy.wait()
    even = info[FAN] == 0
    band = slab // 3

    @pl.loop(0, 6)
    def _(step):
        part = lax.div(step, 3)
        start = lax.rem(step, 3) * band
        near = pl.ds(pl.multiple_of(start, band), band)
        for held, green in ((info[FAN + 1], first), (1 - info[FAN + 1], second)):
            base = held * 2 * slab + part * slab + start
            rows = pl.ds(pl.multiple_of(base, band), band)

            @pl.when(even)
            def _():
                for pair in range(FAN):
                    for column in range(2):
                        at = column * cells + pair * 2 * slab
                        out[info[pair], rows, column * 2 * slab : (column + 1) * 2 * slab] = green[
                            part, near, at : at + 2 * slab
                        ]

            @pl.when(jnp.logical_not(even))
            def _():
                for pair in range(FAN):
                    for column in range(2):
                        low = column * cells + pair * slab
                        high = low + cells // 2
                        left = green[part, near, low : low + slab]
                        right = green[part, near, high : high + slab]
                        out[info[pair], rows, column * 2 * slab : (column + 1) * 2 * slab] = (
                            jnp.concatenate([left, right], 1)
                        )


def loaded(info, own, other):
    slab, cells = own.shape[1], own.shape[2] // 2
    anywhere = pl.BlockSpec(memory_space=pl.ANY)
    return pl.pallas_call(
        load_kernel,
        out_shape=jax.ShapeDtypeStruct((FAN, 4 * slab, 2 * cells // FAN), own.dtype),
        in_specs=[pl.BlockSpec(memory_space=pltpu.SMEM), anywhere, anywhere],
        out_specs=pl.BlockSpec(memory_space=pltpu.VMEM),
        scratch_shapes=[
            pltpu.VMEM(own.shape, own.dtype),
            pltpu.VMEM(own.shape, own.dtype),
            pltpu.SemaphoreType.DMA((2,)),
        ],
        compiler_params=pltpu.CompilerParams(vmem_limit_bytes=16 * 1024 * 1024),
        cost_estimate=pl.CostEstimate(
            flops=0, bytes_accessed=8 * own.size, transcendentals=0
        ),
    )(info, own, other)


def is_live(step):
    layer = lax.axis_index("layer")
    return jnp.logical_or(layer == step, layer == LAYERS - 1 - step)


def product(batch, green, pieces, whole, total, sums):
    cells, lanes = pieces[0].shape
    half = lanes // 2
    for k, piece in enumerate(pieces):
        block = piece[...]
        whole[k, :cells] = block
        whole[k, cells:] = jnp.concatenate([block[:, half:], block[:, :half]], 1)
    rows = total.shape[0] // 2

    @pl.loop(0, 2)
    def _(part):
        at = pl.ds(pl.multiple_of(part * rows, rows), rows)
        terms = [part[at, :] for part in sums]
        for k, r in enumerate(batch):
            terms.append(jnp.dot(green[r, at, :], whole[k], preferred_element_type=jnp.float32))
        total[at, :] = functools.reduce(jnp.add, terms)


def early_kernel(batch, step, green, *refs):
    pieces, sums, (total, whole) = refs[: len(batch)], refs[len(batch) : -2], refs[-2:]

    @pl.when(is_live(step))
    def _():
        product(batch, green, pieces, whole, total, sums)


def late_kernel(batch, step, green, trace, before, sent, earlier, *refs):
    pieces, (after, rounded, whole, rest) = refs[: len(batch)], refs[len(batch) :]
    slab = trace.shape[0] // 2
    half = trace.shape[1] // 2

    @pl.when(is_live(step))
    def _():
        product(batch, green, pieces, whole, rest, (earlier,))
        lane = lax.broadcasted_iota(jnp.int32, (slab, 2 * half), 1)
        for side in range(2):
            rows = slice(side * slab, (side + 1) * slab)
            real = rest[2 * side * slab : (2 * side + 1) * slab, :]
            imag = rest[(2 * side + 1) * slab : (2 * side + 2) * slab, :]
            value = trace[rows, :] + jnp.where(lane < half, real, pltpu.roll(imag, half, 1))
            after[rows, :] = value
            rounded[rows, :] = value.astype(jnp.bfloat16)

    @pl.when(jnp.logical_not(is_live(step)))
    def _():
        after[...] = before[...]
        rounded[...] = sent[...]


def one_step(step, green, trace, before, sent, pieces):
    rows, lanes = trace.shape
    vmem = pl.BlockSpec(memory_space=pltpu.VMEM)
    *early, late = BATCHES
    params = pltpu.CompilerParams(vmem_limit_bytes=8 * 1024 * 1024)

    def cost(batch):
        work = 2 * green.shape[1] * green.shape[2] * lanes * len(batch)
        return pl.CostEstimate(flops=work, bytes_accessed=work // 128, transcendentals=0)

    def held(batch):
        return pltpu.VMEM((len(batch), 2 * rows, lanes), jnp.bfloat16)

    sums = []
    for batch in early:
        total = pl.pallas_call(
            functools.partial(early_kernel, batch, step),
            out_shape=jax.ShapeDtypeStruct((2 * rows, lanes), jnp.float32),
            in_specs=[vmem] * (1 + len(batch) + len(sums)),
            out_specs=vmem,
            scratch_shapes=[held(batch)],
            compiler_params=params,
            cost_estimate=cost(batch),
        )(green, *[pieces[r] for r in batch], *sums)
        sums = [total]
    return pl.pallas_call(
        functools.partial(late_kernel, late, step),
        out_shape=(
            jax.ShapeDtypeStruct((rows, lanes), jnp.float32),
            jax.ShapeDtypeStruct((rows, lanes), jnp.bfloat16),
        ),
        in_specs=[vmem] * (5 + len(late)),
        out_specs=(vmem, vmem),
        scratch_shapes=[held(late), pltpu.VMEM((2 * rows, lanes), jnp.float32)],
        compiler_params=params,
        cost_estimate=cost(late),
    )(green, trace, before, sent, *sums, *[pieces[r] for r in late])


def local(source, wavenumber, green_down, green_up):
    layer = lax.axis_index("layer")
    lat = lax.axis_index("lat")
    low = layer < HALF
    parity = layer & 1
    place = jnp.where(parity == 0, lat >> 2, lat & 1)
    upper = place == 1
    ranks = jnp.asarray(rank_table().reshape(2 * LATS, FAN))
    mine = lax.dynamic_index_in_dim(ranks, parity * LATS + lat, 0, keepdims=False)
    info = jnp.concatenate([mine, jnp.stack([parity, place])])

    own_first = jnp.where(low, green_down[0], green_up[0])
    own_first, source, wavenumber = lax.optimization_barrier((own_first, source, wavenumber))
    other_first = lax.ppermute(own_first, BOTH, INNER_PAIRS)

    traces = relaxed(source[0], wavenumber[0])
    half = traces.shape[2] // 2

    def packed(part):
        columns = slice(part * half, (part + 1) * half)
        return jnp.concatenate([traces[0, :, columns], traces[1, :, columns]], 1)

    keep = jnp.where(upper, packed(1), packed(0))
    give = jnp.where(upper, packed(0), packed(1))
    swapped = lax.ppermute(give, BOTH, PAIRS)
    trace = jnp.where(
        upper, jnp.concatenate([swapped, keep], 0), jnp.concatenate([keep, swapped], 0)
    )
    green_first = loaded(info, own_first, other_first)

    def advance(step, green, before, sent):
        if step == HALF:
            shifted = lax.ppermute(sent, BOTH, straight(step))
            pieces = [lax.ppermute(shifted, BOTH, spread(step, r)) for r in range(FAN)]
        else:
            pieces = [lax.ppermute(sent, BOTH, routes(step, r)) for r in range(FAN)]
        return one_step(step, green, trace, before, sent, pieces)

    slab = traces.shape[1]

    def joined(done):
        held = jnp.where(upper, done[slab:], done[:slab])
        got = lax.ppermute(jnp.where(upper, done[:slab], done[slab:]), BOTH, PAIRS)
        left = jnp.where(upper, got, held)
        right = jnp.where(upper, held, got)
        real = jnp.concatenate([left[:, :half], right[:, :half]], 1)
        imag = jnp.concatenate([left[:, half:], right[:, half:]], 1)
        return jnp.stack([real, imag], 0)

    first, sent = trace, trace.astype(jnp.bfloat16)
    for step in range(1, HALF):
        if step == SWAP:
            down_later, up_later, sent = lax.optimization_barrier((green_down, green_up, sent))
            own_second = jnp.where(low, up_later[0], down_later[0])
            other_second = lax.ppermute(own_second, BOTH, PAIRS)
        if step == HALF - 1:
            green_second = loaded(info, own_second, other_second)
            green_first, green_second = lax.optimization_barrier((green_first, green_second))
        first, sent = advance(step, green_first, first, sent)
    near = joined(first)
    second = trace
    for step in range(HALF, LAYERS):
        second, sent = advance(step, green_second, second, sent)
    far = joined(second)
    down = jnp.where(low, near, far)
    up = jnp.where(low, far, near)
    return (down[None], up[None])


def solution(mesh):
    return jax.shard_map(
        local,
        mesh=mesh,
        in_specs=(
            P("layer", None, "lat", None),
            P("layer", "lat", None),
            P("layer", None, "lat", None),
            P("layer", None, "lat", None),
        ),
        out_specs=(P("layer", None, "lat", None), P("layer", None, "lat", None)),
        check_vma=False,
    )
```

```python
import functools

import jax
import jax.numpy as jnp
import numpy as np
from jax import lax
from jax.experimental import pallas as pl
from jax.experimental.pallas import tpu as pltpu
from jax.sharding import PartitionSpec as P


RELAX = 4
LAYERS = 16
LATS = 8
HALF = LAYERS // 2
BOTH = ("layer", "lat")
SHARED = ((1, 5), (2, 6), (3, 7, 11), (4, 9, 14), (10, 13), (12, 15))
FAN = 4
SWAP = 6
BATCHES = ((3, 1), (0,), (2,))


relax_weight = 0.8
damping = 0.5


def partner_of(layer, lat):
    return lat ^ 4 if layer % 2 == 0 else lat ^ 1


def target_of(layer, lat, r):
    y, z = lat >> 2, lat & 3
    a, b = r >> 1, r & 1
    if layer % 2 == 0:
        return (((z & 1) ^ a) << 2) | (y + 2 * ((z >> 1) ^ b))
    return ((z & 1) << 2) | ((y ^ a) + 2 * ((z >> 1) ^ b))


def edges_of(step):
    return [(step - 1, step), (LAYERS - step, LAYERS - 1 - step)]


def routes(step, r):
    steps = next(group for group in SHARED if step in group)
    edges = [edge for s in steps for edge in edges_of(s)]
    return [
        (src * LATS + j, dst * LATS + target_of(src, j, r)) for src, dst in edges for j in range(LATS)
    ]


def spread(step, r):
    return [
        (dst * LATS + j, dst * LATS + target_of(src, j, r))
        for src, dst in edges_of(step)
        for j in range(LATS)
    ]


def straight(step):
    return [(src * LATS + j, dst * LATS + j) for src, dst in edges_of(step) for j in range(LATS)]


PAIRS = [(l * LATS + j, l * LATS + partner_of(l, j)) for l in range(LAYERS) for j in range(LATS)]


INNER_PAIRS = [pair for pair in PAIRS if 0 < pair[0] // LATS < LAYERS - 1]

MIDDLE = range(4, 12)
MIDDLE_PAIRS = [pair for pair in PAIRS if pair[0] // LATS in MIDDLE]
OUTER_PAIRS = [pair for pair in PAIRS if pair[0] // LATS not in MIDDLE]


def rank_table():
    table = np.zeros((2, LATS, FAN), np.int32)
    for parity in range(2):
        source = 1 - parity
        for j in range(LATS):
            pair = j % 4 if source % 2 == 0 else j // 2
            for r in range(FAN):
                table[parity, target_of(source, j, r), pair] = r
    return table


def padded_2(block, axis, dim, width):
    count = lax.axis_size(axis)
    forward = [(i, i + 1) for i in range(count - 1)]
    backward = [(target, source) for source, target in forward]
    last = lax.slice_in_dim(block, block.shape[dim] - width, None, axis=dim)
    low = lax.ppermute(last, axis, forward)
    high = lax.ppermute(lax.slice_in_dim(block, 0, width, axis=dim), axis, backward)
    return jnp.concatenate([low, block, high], axis=dim)


def relax_step(field, lateral_pad, forcing, diag_real, diag_imag, inverse_real, inverse_imag):
    along = jnp.pad(field, ((0, 0), (0, 0), (1, 1)))
    beside = lateral_pad[:, 2:] + lateral_pad[:, :-2] + along[:, :, 2:] + along[:, :, :-2]
    apply_real = diag_real * field[0] - diag_imag * field[1] - beside[0]
    apply_imag = diag_real * field[1] + diag_imag * field[0] - beside[1]
    res_real = forcing[0] - apply_real
    res_imag = forcing[1] - apply_imag
    step_real = res_real * inverse_real - res_imag * inverse_imag
    step_imag = res_real * inverse_imag + res_imag * inverse_real
    return field + relax_weight * jnp.stack([step_real, step_imag], 0)


def coefficients(wave_sq):
    diag_real = 4.0 - wave_sq
    diag_imag = damping * wave_sq
    denom = diag_real * diag_real + diag_imag * diag_imag
    return (diag_real, diag_imag, diag_real / denom, -diag_imag / denom)


def relaxed(forcing, wave_sq):
    slab = forcing.shape[1]
    width = slab * lax.axis_size("lat")
    stacked = jnp.concatenate([forcing, wave_sq[None]], 0)
    wide = padded_2(stacked.astype(jnp.bfloat16), "lat", 1, RELAX).astype(stacked.dtype)
    wide_forcing = wide[:2]
    diag_real, diag_imag, inverse_real, inverse_imag = coefficients(wide[2])
    position = lax.axis_index("lat") * slab - RELAX + lax.iota(jnp.int32, slab + 2 * RELAX)
    inside = ((position >= 0) & (position < width)).astype(jnp.float32)[None, :, None]
    field = jnp.zeros_like(wide_forcing)
    for _ in range(RELAX):
        padded = jnp.pad(field, ((0, 0), (1, 1), (0, 0)))
        field = (
            relax_step(
                field, padded, wide_forcing, diag_real, diag_imag, inverse_real, inverse_imag
            )
            * inside
        )
    return field[:, RELAX : RELAX + slab]


def load_kernel(info, own, *refs):
    others, (out, first, second, sems) = refs[:-4], refs[-4:]
    slab = first.shape[1]
    cells = first.shape[2] // 2
    near = pltpu.make_async_copy(own, first, sems.at[0])
    near.start()
    for k, other in enumerate(others):

        @pl.when(jnp.logical_or(len(others) == 1, info[FAN + 2] == k))
        def _():
            far = pltpu.make_async_copy(other, second, sems.at[1])
            far.start()
            far.wait()

    near.wait()
    even = info[FAN] == 0
    band = slab // 3

    @pl.loop(0, 6)
    def _(step):
        part = lax.div(step, 3)
        start = lax.rem(step, 3) * band
        near = pl.ds(pl.multiple_of(start, band), band)
        for held, green in ((info[FAN + 1], first), (1 - info[FAN + 1], second)):
            base = held * 2 * slab + part * slab + start
            rows = pl.ds(pl.multiple_of(base, band), band)

            @pl.when(even)
            def _():
                for pair in range(FAN):
                    for column in range(2):
                        at = column * cells + pair * 2 * slab
                        out[info[pair], rows, column * 2 * slab : (column + 1) * 2 * slab] = green[
                            part, near, at : at + 2 * slab
                        ]

            @pl.when(jnp.logical_not(even))
            def _():
                for pair in range(FAN):
                    for column in range(2):
                        low = column * cells + pair * slab
                        high = low + cells // 2
                        left = green[part, near, low : low + slab]
                        right = green[part, near, high : high + slab]
                        out[info[pair], rows, column * 2 * slab : (column + 1) * 2 * slab] = (
                            jnp.concatenate([left, right], 1)
                        )


def loaded(info, own, *others):
    slab, cells = own.shape[1], own.shape[2] // 2
    anywhere = pl.BlockSpec(memory_space=pl.ANY)
    return pl.pallas_call(
        load_kernel,
        out_shape=jax.ShapeDtypeStruct((FAN, 4 * slab, 2 * cells // FAN), own.dtype),
        in_specs=[pl.BlockSpec(memory_space=pltpu.SMEM)] + [anywhere] * (1 + len(others)),
        out_specs=pl.BlockSpec(memory_space=pltpu.VMEM),
        scratch_shapes=[
            pltpu.VMEM(own.shape, own.dtype),
            pltpu.VMEM(own.shape, own.dtype),
            pltpu.SemaphoreType.DMA((2,)),
        ],
        compiler_params=pltpu.CompilerParams(vmem_limit_bytes=16 * 1024 * 1024),
        cost_estimate=pl.CostEstimate(
            flops=0, bytes_accessed=8 * own.size, transcendentals=0
        ),
    )(info, own, *others)


def is_live(step):
    layer = lax.axis_index("layer")
    return jnp.logical_or(layer == step, layer == LAYERS - 1 - step)


def product(batch, green, pieces, whole, total, sums):
    cells, lanes = pieces[0].shape
    half = lanes // 2
    for k, piece in enumerate(pieces):
        block = piece[...]
        whole[k, :cells] = block
        whole[k, cells:] = jnp.concatenate([block[:, half:], block[:, :half]], 1)
    rows = total.shape[0] // 2

    @pl.loop(0, 2)
    def _(part):
        at = pl.ds(pl.multiple_of(part * rows, rows), rows)
        terms = [part[at, :] for part in sums]
        for k, r in enumerate(batch):
            terms.append(jnp.dot(green[r, at, :], whole[k], preferred_element_type=jnp.float32))
        total[at, :] = functools.reduce(jnp.add, terms)


def early_kernel(batch, step, green, *refs):
    pieces, sums, (total, whole) = refs[: len(batch)], refs[len(batch) : -2], refs[-2:]

    @pl.when(is_live(step))
    def _():
        product(batch, green, pieces, whole, total, sums)


def late_kernel(batch, step, green, trace, before, sent, earlier, *refs):
    pieces, (after, rounded, whole, rest) = refs[: len(batch)], refs[len(batch) :]
    slab = trace.shape[0] // 2
    half = trace.shape[1] // 2

    @pl.when(is_live(step))
    def _():
        product(batch, green, pieces, whole, rest, (earlier,))
        lane = lax.broadcasted_iota(jnp.int32, (slab, 2 * half), 1)
        for side in range(2):
            rows = slice(side * slab, (side + 1) * slab)
            real = rest[2 * side * slab : (2 * side + 1) * slab, :]
            imag = rest[(2 * side + 1) * slab : (2 * side + 2) * slab, :]
            value = trace[rows, :] + jnp.where(lane < half, real, pltpu.roll(imag, half, 1))
            after[rows, :] = value
            rounded[rows, :] = value.astype(jnp.bfloat16)

    @pl.when(jnp.logical_not(is_live(step)))
    def _():
        after[...] = before[...]
        rounded[...] = sent[...]


def one_step(step, green, trace, before, sent, pieces):
    rows, lanes = trace.shape
    vmem = pl.BlockSpec(memory_space=pltpu.VMEM)
    *early, late = BATCHES
    params = pltpu.CompilerParams(vmem_limit_bytes=8 * 1024 * 1024)

    def cost(batch):
        work = 2 * green.shape[1] * green.shape[2] * lanes * len(batch)
        return pl.CostEstimate(flops=work, bytes_accessed=work // 128, transcendentals=0)

    def held(batch):
        return pltpu.VMEM((len(batch), 2 * rows, lanes), jnp.bfloat16)

    sums = []
    for batch in early:
        total = pl.pallas_call(
            functools.partial(early_kernel, batch, step),
            out_shape=jax.ShapeDtypeStruct((2 * rows, lanes), jnp.float32),
            in_specs=[vmem] * (1 + len(batch) + len(sums)),
            out_specs=vmem,
            scratch_shapes=[held(batch)],
            compiler_params=params,
            cost_estimate=cost(batch),
        )(green, *[pieces[r] for r in batch], *sums)
        sums = [total]
    return pl.pallas_call(
        functools.partial(late_kernel, late, step),
        out_shape=(
            jax.ShapeDtypeStruct((rows, lanes), jnp.float32),
            jax.ShapeDtypeStruct((rows, lanes), jnp.bfloat16),
        ),
        in_specs=[vmem] * (5 + len(late)),
        out_specs=(vmem, vmem),
        scratch_shapes=[held(late), pltpu.VMEM((2 * rows, lanes), jnp.float32)],
        compiler_params=params,
        cost_estimate=cost(late),
    )(green, trace, before, sent, *sums, *[pieces[r] for r in late])


def local(source, wavenumber, green_down, green_up):
    layer = lax.axis_index("layer")
    lat = lax.axis_index("lat")
    low = layer < HALF
    parity = layer & 1
    place = jnp.where(parity == 0, lat >> 2, lat & 1)
    upper = place == 1
    ranks = jnp.asarray(rank_table().reshape(2 * LATS, FAN))
    mine = lax.dynamic_index_in_dim(ranks, parity * LATS + lat, 0, keepdims=False)
    middle = ((layer >= MIDDLE.start) & (layer < MIDDLE.stop)).astype(jnp.int32)
    info = jnp.concatenate([mine, jnp.stack([parity, place, middle])])

    own_first = jnp.where(low, green_down[0], green_up[0])
    own_first, source, wavenumber = lax.optimization_barrier((own_first, source, wavenumber))
    other_first = lax.ppermute(own_first, BOTH, INNER_PAIRS)

    traces = relaxed(source[0], wavenumber[0])
    half = traces.shape[2] // 2

    def packed(part):
        columns = slice(part * half, (part + 1) * half)
        return jnp.concatenate([traces[0, :, columns], traces[1, :, columns]], 1)

    keep = jnp.where(upper, packed(1), packed(0))
    give = jnp.where(upper, packed(0), packed(1))
    swapped = lax.ppermute(give, BOTH, PAIRS)
    trace = jnp.where(
        upper, jnp.concatenate([swapped, keep], 0), jnp.concatenate([keep, swapped], 0)
    )
    green_first = loaded(info, own_first, other_first)
    down_later, up_later, traces = lax.optimization_barrier((green_down, green_up, traces))
    own_second = jnp.where(low, up_later[0], down_later[0])
    own_second, other_first = lax.optimization_barrier((own_second, other_first))
    other_middle = lax.ppermute(own_second, BOTH, MIDDLE_PAIRS)

    def advance(step, green, before, sent):
        if step == HALF:
            shifted = lax.ppermute(sent, BOTH, straight(step))
            pieces = [lax.ppermute(shifted, BOTH, spread(step, r)) for r in range(FAN)]
        else:
            pieces = [lax.ppermute(sent, BOTH, routes(step, r)) for r in range(FAN)]
        return one_step(step, green, trace, before, sent, pieces)

    slab = traces.shape[1]

    def joined(done):
        held = jnp.where(upper, done[slab:], done[:slab])
        got = lax.ppermute(jnp.where(upper, done[:slab], done[slab:]), BOTH, PAIRS)
        left = jnp.where(upper, got, held)
        right = jnp.where(upper, held, got)
        real = jnp.concatenate([left[:, :half], right[:, :half]], 1)
        imag = jnp.concatenate([left[:, half:], right[:, half:]], 1)
        return jnp.stack([real, imag], 0)

    first, sent = trace, trace.astype(jnp.bfloat16)
    for step in range(1, HALF):
        if step == SWAP:
            own_late, sent = lax.optimization_barrier((own_second, sent))
            other_outer = lax.ppermute(own_late, BOTH, OUTER_PAIRS)
        if step == HALF - 1:
            green_second = loaded(info, own_second, other_outer, other_middle)
            green_first, green_second = lax.optimization_barrier((green_first, green_second))
        first, sent = advance(step, green_first, first, sent)
    near = joined(first)
    second = trace
    for step in range(HALF, LAYERS):
        second, sent = advance(step, green_second, second, sent)
    far = joined(second)
    down = jnp.where(low, near, far)
    up = jnp.where(low, far, near)
    return (down[None], up[None])


def solution(mesh):
    return jax.shard_map(
        local,
        mesh=mesh,
        in_specs=(
            P("layer", None, "lat", None),
            P("layer", "lat", None),
            P("layer", None, "lat", None),
            P("layer", None, "lat", None),
        ),
        out_specs=(P("layer", None, "lat", None), P("layer", None, "lat", None)),
        check_vma=False,
    )
```

```python
import functools

import jax
import jax.numpy as jnp
import numpy as np
from jax import lax
from jax.experimental import pallas as pl
from jax.experimental.pallas import tpu as pltpu
from jax.sharding import PartitionSpec as P


RELAX = 4
LAYERS = 16
LATS = 8
HALF = LAYERS // 2
BOTH = ("layer", "lat")
SHARED = ((1, 5), (2, 6), (3, 7, 11), (4, 9, 14), (10, 13), (12, 15))
RIDERS = {(10, 13): (HALF - 1, HALF), (12, 15): (HALF, HALF - 1)}
FAN = 4
PLACES = (0, 2, 5, 7)
SWAPS = (4, 1, 3)
SWAP = 6
BATCHES = ((3, 2), (1,), (0,))


relax_weight = 0.8
damping = 0.5


def half_of(lat):
    return (lat >> 2) ^ (lat & 1)


def edges_of(step):
    return [(step - 1, step), (LAYERS - step, LAYERS - 1 - step)]


def routes(step, r):
    steps = next(group for group in SHARED if step in group)
    edges = [edge for s in steps for edge in edges_of(s)]
    if steps in RIDERS:
        edges.append(RIDERS[steps])
    return [
        (src * LATS + j, dst * LATS + (j ^ PLACES[r])) for src, dst in edges for j in range(LATS)
    ]


def swap_pairs(k, layers):
    return [(l * LATS + j, l * LATS + (j ^ SWAPS[k])) for l in layers for j in range(LATS)]


ALL = range(LAYERS)
INNER = range(1, LAYERS - 1)


def sources_of(half):
    return [j for j in range(LATS) if half_of(j) == half]


def rank_table():
    return np.array(
        [[PLACES.index(j ^ s) for s in sources_of(half_of(j))] for j in range(LATS)], np.int32
    )


def padded_2(block, axis, dim, width):
    count = lax.axis_size(axis)
    forward = [(i, i + 1) for i in range(count - 1)]
    backward = [(target, source) for source, target in forward]
    last = lax.slice_in_dim(block, block.shape[dim] - width, None, axis=dim)
    low = lax.ppermute(last, axis, forward)
    high = lax.ppermute(lax.slice_in_dim(block, 0, width, axis=dim), axis, backward)
    return jnp.concatenate([low, block, high], axis=dim)


def relax_step(field, lateral_pad, forcing, diag_real, diag_imag, inverse_real, inverse_imag):
    along = jnp.pad(field, ((0, 0), (0, 0), (1, 1)))
    beside = lateral_pad[:, 2:] + lateral_pad[:, :-2] + along[:, :, 2:] + along[:, :, :-2]
    apply_real = diag_real * field[0] - diag_imag * field[1] - beside[0]
    apply_imag = diag_real * field[1] + diag_imag * field[0] - beside[1]
    res_real = forcing[0] - apply_real
    res_imag = forcing[1] - apply_imag
    step_real = res_real * inverse_real - res_imag * inverse_imag
    step_imag = res_real * inverse_imag + res_imag * inverse_real
    return field + relax_weight * jnp.stack([step_real, step_imag], 0)


def coefficients(wave_sq):
    diag_real = 4.0 - wave_sq
    diag_imag = damping * wave_sq
    denom = diag_real * diag_real + diag_imag * diag_imag
    return (diag_real, diag_imag, diag_real / denom, -diag_imag / denom)


def relaxed(forcing, wave_sq):
    slab = forcing.shape[1]
    width = slab * lax.axis_size("lat")
    stacked = jnp.concatenate([forcing, wave_sq[None]], 0)
    wide = padded_2(stacked.astype(jnp.bfloat16), "lat", 1, RELAX).astype(stacked.dtype)
    wide_forcing = wide[:2]
    diag_real, diag_imag, inverse_real, inverse_imag = coefficients(wide[2])
    position = lax.axis_index("lat") * slab - RELAX + lax.iota(jnp.int32, slab + 2 * RELAX)
    inside = ((position >= 0) & (position < width)).astype(jnp.float32)[None, :, None]
    field = jnp.zeros_like(wide_forcing)
    for _ in range(RELAX):
        padded = jnp.pad(field, ((0, 0), (1, 1), (0, 0)))
        field = (
            relax_step(
                field, padded, wide_forcing, diag_real, diag_imag, inverse_real, inverse_imag
            )
            * inside
        )
    return field[:, RELAX : RELAX + slab]


def load_kernel(info, low_green, high_green, *refs):
    others, (out, both, sems) = refs[:-3], refs[-3:]
    slab = both.shape[2]
    cells = both.shape[3] // 2
    third = slab // 3
    near = [
        pltpu.make_async_copy(green, both.at[0], sems.at[0]) for green in (low_green, high_green)
    ]
    low_half = info[FAN + 1] == 1

    @pl.when(low_half)
    def _():
        near[0].start()

    @pl.when(jnp.logical_not(low_half))
    def _():
        near[1].start()

    far = [
        pltpu.make_async_copy(other, both.at[1, :, pl.ds(k * third, third)], sems.at[1 + k])
        for k, other in enumerate(others)
    ]
    for copy in far:
        copy.start()
    near[0].wait()
    for copy in far:
        copy.wait()

    @pl.loop(0, 12)
    def _(step):
        side = lax.div(step, 6)
        part = lax.rem(lax.div(step, 3), 2)
        start = pl.multiple_of(lax.rem(step, 3) * third, third)
        near_rows = pl.ds(start, third)
        rows = pl.ds(pl.multiple_of(step * third, third), third)
        for half in range(2):

            @pl.when(info[FAN] == half)
            def _():
                for k, place in enumerate(sources_of(half)):
                    for column in range(2):
                        at = column * cells
                        cuts = [(at + place * slab, slab)]
                        for n, swap in enumerate(SWAPS):
                            cuts.append((at + (place ^ swap) * slab + n * third, third))
                        wide = [both[side, part, near_rows, low : low + size] for low, size in cuts]
                        columns = slice(column * 2 * slab, (column + 1) * 2 * slab)
                        out[info[k], rows, columns] = jnp.concatenate(wide, 1)


def loaded(info, low_green, high_green, others):
    _, slab, width = low_green.shape
    dtype = low_green.dtype
    anywhere = pl.BlockSpec(memory_space=pltpu.HBM)
    return pl.pallas_call(
        load_kernel,
        out_shape=jax.ShapeDtypeStruct((FAN, 4 * slab, width // FAN), dtype),
        in_specs=[pl.BlockSpec(memory_space=pltpu.SMEM)] + [anywhere] * (2 + len(others)),
        out_specs=pl.BlockSpec(memory_space=pltpu.VMEM),
        scratch_shapes=[
            pltpu.VMEM((2, *low_green.shape), dtype),
            pltpu.SemaphoreType.DMA((1 + len(SWAPS),)),
        ],
        compiler_params=pltpu.CompilerParams(vmem_limit_bytes=16 * 1024 * 1024),
        cost_estimate=pl.CostEstimate(
            flops=0, bytes_accessed=8 * low_green.size, transcendentals=0
        ),
    )(info, low_green, high_green, *others)


def is_live(step):
    layer = lax.axis_index("layer")
    return jnp.logical_or(layer == step, layer == LAYERS - 1 - step)


def product(batch, green, pieces, whole, total, sums):
    cells, lanes = pieces[0].shape
    half = lanes // 2
    for k, piece in enumerate(pieces):
        block = piece[...]
        whole[k, :cells] = block
        whole[k, cells:] = jnp.concatenate([block[:, half:], block[:, :half]], 1)
    rows = total.shape[0] // 2

    @pl.loop(0, 2)
    def _(part):
        at = pl.ds(pl.multiple_of(part * rows, rows), rows)
        terms = [part[at, :] for part in sums]
        for k, r in enumerate(batch):
            terms.append(jnp.dot(green[r, at, :], whole[k], preferred_element_type=jnp.float32))
        total[at, :] = functools.reduce(jnp.add, terms)


def early_kernel(batch, step, green, *refs):
    pieces, sums, (total, whole) = refs[: len(batch)], refs[len(batch) : -2], refs[-2:]

    @pl.when(is_live(step))
    def _():
        product(batch, green, pieces, whole, total, sums)


def late_kernel(batch, step, green, trace, before, sent, earlier, *refs):
    pieces, (after, rounded, whole, rest) = refs[: len(batch)], refs[len(batch) :]
    slab = trace.shape[0] // 2
    half = trace.shape[1] // 2

    @pl.when(is_live(step))
    def _():
        product(batch, green, pieces, whole, rest, (earlier,))
        lane = lax.broadcasted_iota(jnp.int32, (slab, 2 * half), 1)
        for side in range(2):
            rows = slice(side * slab, (side + 1) * slab)
            real = rest[2 * side * slab : (2 * side + 1) * slab, :]
            imag = rest[(2 * side + 1) * slab : (2 * side + 2) * slab, :]
            value = trace[rows, :] + jnp.where(lane < half, real, pltpu.roll(imag, half, 1))
            after[rows, :] = value
            rounded[rows, :] = value.astype(jnp.bfloat16)

    @pl.when(jnp.logical_not(is_live(step)))
    def _():
        after[...] = before[...]
        rounded[...] = sent[...]


def one_step(step, green, trace, before, sent, pieces):
    rows, lanes = trace.shape
    vmem = pl.BlockSpec(memory_space=pltpu.VMEM)
    *early, late = BATCHES
    params = pltpu.CompilerParams(vmem_limit_bytes=8 * 1024 * 1024)

    def cost(batch):
        work = 2 * green.shape[1] * green.shape[2] * lanes * len(batch)
        return pl.CostEstimate(flops=work, bytes_accessed=work // 128, transcendentals=0)

    def held(batch):
        return pltpu.VMEM((len(batch), 2 * rows, lanes), jnp.bfloat16)

    sums = []
    for batch in early:
        total = pl.pallas_call(
            functools.partial(early_kernel, batch, step),
            out_shape=jax.ShapeDtypeStruct((2 * rows, lanes), jnp.float32),
            in_specs=[vmem] * (1 + len(batch) + len(sums)),
            out_specs=vmem,
            scratch_shapes=[held(batch)],
            compiler_params=params,
            cost_estimate=cost(batch),
        )(green, *[pieces[r] for r in batch], *sums)
        sums = [total]
    return pl.pallas_call(
        functools.partial(late_kernel, late, step),
        out_shape=(
            jax.ShapeDtypeStruct((rows, lanes), jnp.float32),
            jax.ShapeDtypeStruct((rows, lanes), jnp.bfloat16),
        ),
        in_specs=[vmem] * (5 + len(late)),
        out_specs=(vmem, vmem),
        scratch_shapes=[held(late), pltpu.VMEM((2 * rows, lanes), jnp.float32)],
        compiler_params=params,
        cost_estimate=cost(late),
    )(green, trace, before, sent, *sums, *[pieces[r] for r in late])


def thirds(rows):
    size = rows.shape[-2] // 3
    return [rows[..., k * size : (k + 1) * size, :] for k in range(3)]


def local(source, wavenumber, green_down, green_up):
    layer = lax.axis_index("layer")
    lat = lax.axis_index("lat")
    low = layer < HALF
    place = (lat >> 2) ^ (lat & 1)
    upper = place == 1
    mine = lax.dynamic_index_in_dim(jnp.asarray(rank_table()), lat, 0, keepdims=False)
    info = jnp.concatenate([mine, jnp.stack([place, low.astype(jnp.int32)])])
    down, up = green_down[0], green_up[0]

    def swapped(parts, layers):
        return [lax.ppermute(x, BOTH, swap_pairs(k, layers)) for k, x in enumerate(parts)]

    given = [jnp.where(low, a, b) for a, b in zip(thirds(down), thirds(up))]
    given, source, wavenumber = lax.optimization_barrier((given, source, wavenumber))
    others_first = swapped(given, INNER)

    traces = relaxed(source[0], wavenumber[0])
    half = traces.shape[2] // 2
    slab = traces.shape[1]

    def packed(part):
        columns = slice(part * half, (part + 1) * half)
        return jnp.concatenate([traces[0, :, columns], traces[1, :, columns]], 1)

    keep = jnp.where(upper, packed(1), packed(0))
    give = jnp.where(upper, packed(0), packed(1))
    trace = jnp.concatenate([keep, *swapped(thirds(give), ALL)], 0)
    green_first = loaded(info, down, up, others_first)
    down_later, up_later, traces = lax.optimization_barrier((down, up, traces))
    given = [jnp.where(low, b, a) for a, b in zip(thirds(down_later), thirds(up_later))]

    def advance(step, green, before, sent):
        if step == HALF:
            ways = [[lax.ppermute(sent, BOTH, routes(s, r)) for r in range(FAN)] for s in (10, 12)]
            pieces = [a + b for a, b in zip(*ways)]
        else:
            pieces = [lax.ppermute(sent, BOTH, routes(step, r)) for r in range(FAN)]
        return one_step(step, green, trace, before, sent, pieces)

    def joined(done):
        held = done[:slab]
        got = jnp.concatenate(swapped(thirds(done[slab:]), ALL), 0)
        left = jnp.where(upper, got, held)
        right = jnp.where(upper, held, got)
        real = jnp.concatenate([left[:, :half], right[:, :half]], 1)
        imag = jnp.concatenate([left[:, half:], right[:, half:]], 1)
        return jnp.stack([real, imag], 0)

    first, sent = trace, trace.astype(jnp.bfloat16)
    for step in range(1, HALF):
        if step == SWAP:
            given, sent = lax.optimization_barrier((given, sent))
            others_second = swapped(given, ALL)
        if step == HALF - 1:
            green_second = loaded(info, up, down, others_second)
            green_first, green_second = lax.optimization_barrier((green_first, green_second))
        first, sent = advance(step, green_first, first, sent)
    near = joined(first)
    second = trace
    for step in range(HALF, LAYERS):
        second, sent = advance(step, green_second, second, sent)
    far = joined(second)
    down_trace = jnp.where(low, near, far)
    up_trace = jnp.where(low, far, near)
    return (down_trace[None], up_trace[None])


def solution(mesh):
    return jax.shard_map(
        local,
        mesh=mesh,
        in_specs=(
            P("layer", None, "lat", None),
            P("layer", "lat", None),
            P("layer", None, "lat", None),
            P("layer", None, "lat", None),
        ),
        out_specs=(P("layer", None, "lat", None), P("layer", None, "lat", None)),
        check_vma=False,
    )
```

```python
import functools

import jax
import jax.numpy as jnp
import numpy as np
from jax import lax
from jax.experimental import pallas as pl
from jax.experimental.pallas import tpu as pltpu
from jax.sharding import PartitionSpec as P


RELAX = 4
LAYERS = 16
LATS = 8
HALF = LAYERS // 2
BOTH = ("layer", "lat")
SHARED = ((1, 9), (2, 10), (3, 15), (4, 14), (5, 13), (6, 12), (7, 11))
RIDERS = {(3, 15): (HALF - 1, HALF), (4, 14): (HALF, HALF - 1)}
FAN = 4
SWAP = 7
BATCHES = ((3, 1), (0,), (2,))


relax_weight = 0.8
damping = 0.5


def partner_of(layer, lat):
    return lat ^ 4 if layer % 2 == 0 else lat ^ 1


def target_of(layer, lat, r):
    y, z = lat >> 2, lat & 3
    a, b = r >> 1, r & 1
    if layer % 2 == 0:
        return (((z & 1) ^ a) << 2) | (y + 2 * ((z >> 1) ^ b))
    return ((z & 1) << 2) | ((y ^ a) + 2 * ((z >> 1) ^ b))


def edges_of(step):
    return [(step - 1, step), (LAYERS - step, LAYERS - 1 - step)]


def routes(step, r):
    steps = next(group for group in SHARED if step in group)
    edges = [edge for s in steps for edge in edges_of(s)]
    if steps in RIDERS:
        edges.append(RIDERS[steps])
    return [
        (src * LATS + j, dst * LATS + target_of(src, j, r)) for src, dst in edges for j in range(LATS)
    ]


PAIRS = [(l * LATS + j, l * LATS + partner_of(l, j)) for l in range(LAYERS) for j in range(LATS)]


INNER_PAIRS = [pair for pair in PAIRS if 0 < pair[0] // LATS < LAYERS - 1]

MIDDLE = range(4, 12)
MIDDLE_PAIRS = [pair for pair in PAIRS if pair[0] // LATS in MIDDLE]
OUTER_PAIRS = [pair for pair in PAIRS if pair[0] // LATS not in MIDDLE]


def rank_table():
    table = np.zeros((2, LATS, FAN), np.int32)
    for parity in range(2):
        source = 1 - parity
        for j in range(LATS):
            pair = j % 4 if source % 2 == 0 else j // 2
            for r in range(FAN):
                table[parity, target_of(source, j, r), pair] = r
    return table


def padded_2(block, axis, dim, width):
    count = lax.axis_size(axis)
    forward = [(i, i + 1) for i in range(count - 1)]
    backward = [(target, source) for source, target in forward]
    last = lax.slice_in_dim(block, block.shape[dim] - width, None, axis=dim)
    low = lax.ppermute(last, axis, forward)
    high = lax.ppermute(lax.slice_in_dim(block, 0, width, axis=dim), axis, backward)
    return jnp.concatenate([low, block, high], axis=dim)


def relax_step(field, lateral_pad, forcing, diag_real, diag_imag, inverse_real, inverse_imag):
    along = jnp.pad(field, ((0, 0), (0, 0), (1, 1)))
    beside = lateral_pad[:, 2:] + lateral_pad[:, :-2] + along[:, :, 2:] + along[:, :, :-2]
    apply_real = diag_real * field[0] - diag_imag * field[1] - beside[0]
    apply_imag = diag_real * field[1] + diag_imag * field[0] - beside[1]
    res_real = forcing[0] - apply_real
    res_imag = forcing[1] - apply_imag
    step_real = res_real * inverse_real - res_imag * inverse_imag
    step_imag = res_real * inverse_imag + res_imag * inverse_real
    return field + relax_weight * jnp.stack([step_real, step_imag], 0)


def coefficients(wave_sq):
    diag_real = 4.0 - wave_sq
    diag_imag = damping * wave_sq
    denom = diag_real * diag_real + diag_imag * diag_imag
    return (diag_real, diag_imag, diag_real / denom, -diag_imag / denom)


def relaxed(forcing, wave_sq):
    slab = forcing.shape[1]
    width = slab * lax.axis_size("lat")
    stacked = jnp.concatenate([forcing, wave_sq[None]], 0)
    wide = padded_2(stacked.astype(jnp.bfloat16), "lat", 1, RELAX).astype(stacked.dtype)
    wide_forcing = wide[:2]
    diag_real, diag_imag, inverse_real, inverse_imag = coefficients(wide[2])
    position = lax.axis_index("lat") * slab - RELAX + lax.iota(jnp.int32, slab + 2 * RELAX)
    inside = ((position >= 0) & (position < width)).astype(jnp.float32)[None, :, None]
    field = jnp.zeros_like(wide_forcing)
    for _ in range(RELAX):
        padded = jnp.pad(field, ((0, 0), (1, 1), (0, 0)))
        field = (
            relax_step(
                field, padded, wide_forcing, diag_real, diag_imag, inverse_real, inverse_imag
            )
            * inside
        )
    return field[:, RELAX : RELAX + slab]


def load_kernel(info, own, *refs):
    others, (out, first, second, sems) = refs[:-4], refs[-4:]
    slab = first.shape[1]
    cells = first.shape[2] // 2
    near = pltpu.make_async_copy(own, first, sems.at[0])
    near.start()
    for k, other in enumerate(others):

        @pl.when(jnp.logical_or(len(others) == 1, info[FAN + 2] == k))
        def _():
            far = pltpu.make_async_copy(other, second, sems.at[1])
            far.start()
            far.wait()

    near.wait()
    even = info[FAN] == 0
    band = slab // 3

    @pl.loop(0, 6)
    def _(step):
        part = lax.div(step, 3)
        start = lax.rem(step, 3) * band
        near = pl.ds(pl.multiple_of(start, band), band)
        for held, green in ((info[FAN + 1], first), (1 - info[FAN + 1], second)):
            base = held * 2 * slab + part * slab + start
            rows = pl.ds(pl.multiple_of(base, band), band)

            @pl.when(even)
            def _():
                for pair in range(FAN):
                    for column in range(2):
                        at = column * cells + pair * 2 * slab
                        out[info[pair], rows, column * 2 * slab : (column + 1) * 2 * slab] = green[
                            part, near, at : at + 2 * slab
                        ]

            @pl.when(jnp.logical_not(even))
            def _():
                for pair in range(FAN):
                    for column in range(2):
                        low = column * cells + pair * slab
                        high = low + cells // 2
                        left = green[part, near, low : low + slab]
                        right = green[part, near, high : high + slab]
                        out[info[pair], rows, column * 2 * slab : (column + 1) * 2 * slab] = (
                            jnp.concatenate([left, right], 1)
                        )


def loaded(info, own, *others):
    slab, cells = own.shape[1], own.shape[2] // 2
    anywhere = pl.BlockSpec(memory_space=pl.ANY)
    return pl.pallas_call(
        load_kernel,
        out_shape=jax.ShapeDtypeStruct((FAN, 4 * slab, 2 * cells // FAN), own.dtype),
        in_specs=[pl.BlockSpec(memory_space=pltpu.SMEM)] + [anywhere] * (1 + len(others)),
        out_specs=pl.BlockSpec(memory_space=pltpu.VMEM),
        scratch_shapes=[
            pltpu.VMEM(own.shape, own.dtype),
            pltpu.VMEM(own.shape, own.dtype),
            pltpu.SemaphoreType.DMA((2,)),
        ],
        compiler_params=pltpu.CompilerParams(vmem_limit_bytes=16 * 1024 * 1024),
        cost_estimate=pl.CostEstimate(
            flops=0, bytes_accessed=8 * own.size, transcendentals=0
        ),
    )(info, own, *others)


def is_live(step):
    layer = lax.axis_index("layer")
    return jnp.logical_or(layer == step, layer == LAYERS - 1 - step)


def product(batch, green, pieces, whole, total, sums):
    cells, lanes = pieces[0].shape
    half = lanes // 2
    for k, piece in enumerate(pieces):
        block = piece[...]
        whole[k, :cells] = block
        whole[k, cells:] = jnp.concatenate([block[:, half:], block[:, :half]], 1)
    rows = total.shape[0] // 2

    @pl.loop(0, 2)
    def _(part):
        at = pl.ds(pl.multiple_of(part * rows, rows), rows)
        terms = [part[at, :] for part in sums]
        for k, r in enumerate(batch):
            terms.append(jnp.dot(green[r, at, :], whole[k], preferred_element_type=jnp.float32))
        total[at, :] = functools.reduce(jnp.add, terms)


def early_kernel(batch, step, green, *refs):
    pieces, sums, (total, whole) = refs[: len(batch)], refs[len(batch) : -2], refs[-2:]

    @pl.when(is_live(step))
    def _():
        product(batch, green, pieces, whole, total, sums)


def late_kernel(batch, step, green, trace, before, sent, earlier, *refs):
    pieces, (after, rounded, whole, rest) = refs[: len(batch)], refs[len(batch) :]
    slab = trace.shape[0] // 2
    half = trace.shape[1] // 2

    @pl.when(is_live(step))
    def _():
        product(batch, green, pieces, whole, rest, (earlier,))
        lane = lax.broadcasted_iota(jnp.int32, (slab, 2 * half), 1)
        for side in range(2):
            rows = slice(side * slab, (side + 1) * slab)
            real = rest[2 * side * slab : (2 * side + 1) * slab, :]
            imag = rest[(2 * side + 1) * slab : (2 * side + 2) * slab, :]
            value = trace[rows, :] + jnp.where(lane < half, real, pltpu.roll(imag, half, 1))
            after[rows, :] = value
            rounded[rows, :] = value.astype(jnp.bfloat16)

    @pl.when(jnp.logical_not(is_live(step)))
    def _():
        after[...] = before[...]
        rounded[...] = sent[...]


def one_step(step, green, trace, before, sent, pieces):
    rows, lanes = trace.shape
    vmem = pl.BlockSpec(memory_space=pltpu.VMEM)
    *early, late = BATCHES
    params = pltpu.CompilerParams(vmem_limit_bytes=8 * 1024 * 1024)

    def cost(batch):
        work = 2 * green.shape[1] * green.shape[2] * lanes * len(batch)
        return pl.CostEstimate(flops=work, bytes_accessed=work // 128, transcendentals=0)

    def held(batch):
        return pltpu.VMEM((len(batch), 2 * rows, lanes), jnp.bfloat16)

    sums = []
    for batch in early:
        total = pl.pallas_call(
            functools.partial(early_kernel, batch, step),
            out_shape=jax.ShapeDtypeStruct((2 * rows, lanes), jnp.float32),
            in_specs=[vmem] * (1 + len(batch) + len(sums)),
            out_specs=vmem,
            scratch_shapes=[held(batch)],
            compiler_params=params,
            cost_estimate=cost(batch),
        )(green, *[pieces[r] for r in batch], *sums)
        sums = [total]
    return pl.pallas_call(
        functools.partial(late_kernel, late, step),
        out_shape=(
            jax.ShapeDtypeStruct((rows, lanes), jnp.float32),
            jax.ShapeDtypeStruct((rows, lanes), jnp.bfloat16),
        ),
        in_specs=[vmem] * (5 + len(late)),
        out_specs=(vmem, vmem),
        scratch_shapes=[held(late), pltpu.VMEM((2 * rows, lanes), jnp.float32)],
        compiler_params=params,
        cost_estimate=cost(late),
    )(green, trace, before, sent, *sums, *[pieces[r] for r in late])


def local(source, wavenumber, green_down, green_up):
    layer = lax.axis_index("layer")
    lat = lax.axis_index("lat")
    low = layer < HALF
    parity = layer & 1
    place = jnp.where(parity == 0, lat >> 2, lat & 1)
    upper = place == 1
    ranks = jnp.asarray(rank_table().reshape(2 * LATS, FAN))
    mine = lax.dynamic_index_in_dim(ranks, parity * LATS + lat, 0, keepdims=False)
    middle = ((layer >= MIDDLE.start) & (layer < MIDDLE.stop)).astype(jnp.int32)
    info = jnp.concatenate([mine, jnp.stack([parity, place, middle])])

    own_first = jnp.where(low, green_down[0], green_up[0])
    own_first, source, wavenumber = lax.optimization_barrier((own_first, source, wavenumber))
    other_first = lax.ppermute(own_first, BOTH, INNER_PAIRS)

    traces = relaxed(source[0], wavenumber[0])
    half = traces.shape[2] // 2

    def packed(part):
        columns = slice(part * half, (part + 1) * half)
        return jnp.concatenate([traces[0, :, columns], traces[1, :, columns]], 1)

    keep = jnp.where(upper, packed(1), packed(0))
    give = jnp.where(upper, packed(0), packed(1))
    swapped = lax.ppermute(give, BOTH, PAIRS)
    trace = jnp.where(
        upper, jnp.concatenate([swapped, keep], 0), jnp.concatenate([keep, swapped], 0)
    )
    green_first = loaded(info, own_first, other_first)
    down_later, up_later, traces = lax.optimization_barrier((green_down, green_up, traces))
    own_second = jnp.where(low, up_later[0], down_later[0])
    own_second, other_first = lax.optimization_barrier((own_second, other_first))
    other_middle = lax.ppermute(own_second, BOTH, MIDDLE_PAIRS)

    def advance(step, green, before, sent):
        if step == HALF:
            ahead = [lax.ppermute(sent, BOTH, routes(3, r)) for r in range(FAN)]
            back = [lax.ppermute(sent, BOTH, routes(4, r)) for r in range(FAN)]
            pieces = [a + b for a, b in zip(ahead, back)]
        else:
            pieces = [lax.ppermute(sent, BOTH, routes(step, r)) for r in range(FAN)]
        return one_step(step, green, trace, before, sent, pieces)

    slab = traces.shape[1]

    def joined(done):
        held = jnp.where(upper, done[slab:], done[:slab])
        got = lax.ppermute(jnp.where(upper, done[:slab], done[slab:]), BOTH, PAIRS)
        left = jnp.where(upper, got, held)
        right = jnp.where(upper, held, got)
        real = jnp.concatenate([left[:, :half], right[:, :half]], 1)
        imag = jnp.concatenate([left[:, half:], right[:, half:]], 1)
        return jnp.stack([real, imag], 0)

    first, sent = trace, trace.astype(jnp.bfloat16)
    for step in range(1, HALF):
        if step == SWAP:
            own_late, sent = lax.optimization_barrier((own_second, sent))
            other_outer = lax.ppermute(own_late, BOTH, OUTER_PAIRS)
        if step == HALF - 1:
            green_second = loaded(info, own_second, other_outer, other_middle)
            green_first, green_second = lax.optimization_barrier((green_first, green_second))
        first, sent = advance(step, green_first, first, sent)
    near = joined(first)
    second = trace
    for step in range(HALF, LAYERS):
        second, sent = advance(step, green_second, second, sent)
    far = joined(second)
    down = jnp.where(low, near, far)
    up = jnp.where(low, far, near)
    return (down[None], up[None])


def solution(mesh):
    return jax.shard_map(
        local,
        mesh=mesh,
        in_specs=(
            P("layer", None, "lat", None),
            P("layer", "lat", None),
            P("layer", None, "lat", None),
            P("layer", None, "lat", None),
        ),
        out_specs=(P("layer", None, "lat", None), P("layer", None, "lat", None)),
        check_vma=False,
    )
```
